256 devices in a mesh: dp: 32 (over x, y, core), ctx: 8 (over z).
Axes of the slice: x: 4, y: 4, z: 8, core: 2. Of those that a mesh axis runs over, the one named last changes fastest.
Arguments:
- cotangent: bfloat16 [32, 4096, 8192], P('dp', 'ctx'), may hold values from -6 to 6
- out_weight: bfloat16 [256, 8192], P(None, 'ctx'), may hold values from -0.0625 to 0.0625
- head_input: bfloat16 [32, 4096, 256], P('dp', 'ctx'), may hold values from -6 to 6
- injector: bfloat16 [32, 4096, 128], P('dp', 'ctx'), may hold values from -0.59765625 to 0.59765625
- readout: bfloat16 [32, 4096, 128], P('dp', 'ctx'), may hold values from -0.59765625 to 0.59765625
- decay_code: int32 [32, 4096, 2], P('dp', 'ctx'), may hold values from 1 to 40960
- decay_rate: float32 [2], replicated, may hold values from 4.8828125e-06 to 0.0061035156
- start_state: float32 [32, 8, 2, 128, 128], P('dp', 'ctx'), may hold values from -6 to 6
Outputs:
- gradient_input: bfloat16 [32, 4096, 256], P('dp', 'ctx')
- gradient_injector: float32 [32, 4096, 128], P('dp', 'ctx')
- gradient_readout: float32 [32, 4096, 128], P('dp', 'ctx')
- gradient_weight: float32 [256, 8192], P('ctx', 'dp')
- gradient_rate: float32 [2], replicated
The draws below stay inside these ranges and needn't reach their ends.
All inputs are finite; a program needn't handle non-finite values.
Results may differ from the reference program's by a relative error of at most 0.0049.
Values may be sent and summed in bfloat16 or wider, within the bound.
No kernel may reach another device: no remote copies, remote signals or barrier semaphores. Data moves between devices by JAX's collectives and lax.ppermute only.
A program may use at most 128 MiB of HBM per device.

```python
import math
import jax
import jax.numpy as jnp
from jax import lax

D = 8192
P_SIZE = 128
N = 128
H = 2
S_DEV = 512
SEQUENCE_COUNT = 32
SEQUENCE_LENGTH = 4096
HP = 256
N_CTX = 8


def draw_decay_code(key, part):
    key_base = jax.random.fold_in(key, 11)
    key_unit = jax.random.fold_in(key, 12)
    spike_key = jax.random.fold_in(key, 13)
    base_level = jax.random.randint(key_base, (SEQUENCE_COUNT, SEQUENCE_LENGTH // S_DEV, 1, H), 2, 9)
    base_level = jnp.broadcast_to(base_level, (SEQUENCE_COUNT, SEQUENCE_LENGTH // S_DEV, S_DEV, H)).reshape(SEQUENCE_COUNT, SEQUENCE_LENGTH, H)
    uniform_bits = jax.random.randint(key_unit, (SEQUENCE_COUNT, SEQUENCE_LENGTH, H), 0, 1 << 20)
    encoded_values = 1 + uniform_bits % (2 * base_level)
    location_list = jax.random.randint(spike_key, (SEQUENCE_COUNT, 3, 1), 0, SEQUENCE_LENGTH)
    token_position = lax.broadcasted_iota(jnp.int32, (SEQUENCE_COUNT, 3, SEQUENCE_LENGTH), 2)
    spike_mask = jnp.any(token_position == location_list, axis=1)
    return jnp.where(spike_mask[:, :, None], 10 * SEQUENCE_LENGTH, encoded_values).astype(jnp.int32)


def draw_decay_rate(key, part):
    low_end, high_end = (0.02, 25.0)
    spread = jax.random.uniform(key, (H,), jnp.float32, math.log(low_end), math.log(high_end))
    return (jnp.exp(spread) / SEQUENCE_LENGTH).astype(jnp.float32)


def raised(entries, key, source, target, blocks, factor):
    def block_of(dim):
        return (jnp.arange(entries.shape[dim]) // (entries.shape[dim] // blocks)).reshape((-1,) + (1,) * (entries.ndim - 1 - dim))

    first = jax.random.permutation(key, blocks)[block_of(target)]
    other_side = (block_of(target) + blocks // 2) % blocks
    return jnp.where((block_of(source) == first) | (block_of(source) == other_side), factor * entries, entries)


def level_of(stream_key, dims, split, low, top_value):
    def one(axis_at, blocks):
        steps = jax.random.uniform(jax.random.fold_in(jax.random.fold_in(stream_key, 6), axis_at), (blocks,), jnp.float32, low / len(split), top_value / len(split))
        return jnp.repeat(jnp.exp(steps), dims[axis_at] // blocks).reshape((-1,) + (1,) * (len(dims) - axis_at - 1))

    level = one(*split[0])
    for cut in split[1:]:
        level = level * one(*cut)
    return level


def noise(own_key, shape, width, reach, cuts=(), held_as=jnp.bfloat16):
    drawn = width * jax.random.normal(own_key, shape, jnp.float32)
    if cuts:
        drawn = drawn * level_of(own_key, shape, cuts, -0.22, 0.18)
    return jnp.clip(drawn, -reach, reach).astype(held_as)


def bell_draw_with(own_key, dims, scale, most, cuts, heavy, kind=jnp.bfloat16):
    result = scale * jax.random.normal(own_key, dims, jnp.float32)
    if cuts:
        result = result * level_of(own_key, dims, cuts, -0.22, 0.18)
    return jnp.clip(raised(result, jax.random.fold_in(own_key, 3), *heavy), -most, most).astype(kind)


def setup_inputs(seed: int = 0) -> dict:
    key_list = jax.random.split(jax.random.key(seed), 9)
    cotangent = bell_draw_with(key_list[0], (SEQUENCE_COUNT, SEQUENCE_LENGTH, D), 1.0, 6.0, ((0, 32), (1, 8)), (0, 2, 32, 2.75))
    out_weight = noise(key_list[1], (HP, D), D ** -0.5, 0.0625, ((1, 8),))
    head_input = noise(key_list[2], (SEQUENCE_COUNT, SEQUENCE_LENGTH, HP), 1.0, 6.0, ((0, 32), (1, 8)))
    injector = noise(key_list[3], (SEQUENCE_COUNT, SEQUENCE_LENGTH, N), 0.1, 0.59765625, ((0, 32), (1, 8)))
    readout = noise(key_list[4], (SEQUENCE_COUNT, SEQUENCE_LENGTH, N), 0.1, 0.59765625, ((0, 32), (1, 8)))
    decay_code = draw_decay_code(jax.random.fold_in(key_list[8], 71), 0)
    decay_rate = draw_decay_rate(jax.random.fold_in(key_list[8], 71), 0)
    start_state = noise(key_list[7], (SEQUENCE_COUNT, N_CTX, H, P_SIZE, N), 1.0, 6.0, ((0, 32), (1, 8)), jnp.float32)
    return dict(cotangent=cotangent, out_weight=out_weight, head_input=head_input, injector=injector, readout=readout, decay_code=decay_code, decay_rate=decay_rate, start_state=start_state)


precise = lax.Precision.HIGHEST


def decay_table(log_decay):
    cumulative = jnp.cumsum(log_decay, axis=0)
    length = log_decay.shape[0]
    row_index = lax.broadcasted_iota(jnp.int32, (length, length), 0)
    col_index = lax.broadcasted_iota(jnp.int32, (length, length), 1)
    causal = (row_index >= col_index)[None]
    spread = cumulative.T[:, :, None] - cumulative.T[:, None, :]
    weights = jnp.where(causal, jnp.exp(jnp.where(causal, spread, 0.0)), 0.0)
    return cumulative, weights


def forward_shard(head_input, injector, readout, log_decay, start_state):
    length, heads_count = log_decay.shape
    cumulative, weights = decay_table(log_decay)
    intersection = jnp.dot(readout, injector.T, preferred_element_type=jnp.float32)
    mixing = intersection[None] * weights
    inputs_heads = head_input.reshape(length, heads_count, -1).astype(jnp.float32)
    within = jnp.einsum("hts,shp->thp", mixing, inputs_heads, precision=precise)
    carried = jnp.einsum("tn,hpn->thp", readout.astype(jnp.float32), start_state, precision=precise)
    outputs = within + jnp.exp(cumulative)[:, :, None] * carried
    return outputs.reshape(length, -1).astype(jnp.bfloat16)


def chain_piece(readout, output_grad, log_decay):
    length, heads_count = log_decay.shape
    cumulative = jnp.cumsum(log_decay, axis=0)
    grad_heads = output_grad.reshape(length, heads_count, -1).astype(jnp.float32)
    scaled = jnp.exp(cumulative)[:, :, None] * readout.astype(jnp.float32)[:, None, :]
    adjoint = jnp.einsum("thp,thn->hpn", grad_heads, scaled, precision=precise)
    return jnp.exp(cumulative[-1]), adjoint


def backward_shard(head_input, injector, readout, output_grad, log_decay, start_state, incoming):
    length, heads_count = log_decay.shape
    cumulative, weights = decay_table(log_decay)
    inputs_heads = head_input.reshape(length, heads_count, -1).astype(jnp.float32)
    grad_heads = output_grad.reshape(length, heads_count, -1).astype(jnp.float32)
    inject_float = injector.astype(jnp.float32)
    read_float = readout.astype(jnp.float32)
    intersection = jnp.dot(readout, injector.T, preferred_element_type=jnp.float32)
    mixing = intersection[None] * weights
    to_end = jnp.exp(cumulative[-1][None, :] - cumulative)
    from_start = jnp.exp(cumulative)
    entering = jnp.einsum("sn,hpn->shp", inject_float, incoming, precision=precise)
    grad_input = jnp.einsum("hts,thp->shp", mixing, grad_heads, precision=precise) + to_end[:, :, None] * entering
    pairing = jnp.einsum("thp,shp->hts", grad_heads, inputs_heads, precision=precise) * weights
    through_start = jnp.einsum("thp,hpn->thn", grad_heads, start_state, precision=precise)
    grad_read = jnp.einsum("hts,sn->tn", pairing, inject_float, precision=precise)
    grad_read = grad_read + jnp.einsum("th,thn->tn", from_start, through_start, precision=precise)
    input_state = jnp.einsum("shp,hpn->shn", inputs_heads, incoming, precision=precise)
    grad_inject = jnp.einsum("hts,tn->sn", pairing, read_float, precision=precise)
    grad_inject = grad_inject + jnp.einsum("sh,shn->sn", to_end, input_state, precision=precise)
    products = intersection[None] * pairing
    carried = jnp.einsum("tn,hpn->thp", read_float, start_state, precision=precise) * from_start[:, :, None]
    reaching = to_end * jnp.einsum("shn,sn->sh", input_state, inject_float, precision=precise)
    end_term = from_start[-1] * jnp.einsum("hpn,hpn->h", incoming, start_state, precision=precise) + jnp.sum(reaching, axis=0)
    cumul_grad = jnp.sum(products, axis=2).T - jnp.sum(products, axis=1).T
    cumul_grad = cumul_grad + jnp.sum(grad_heads * carried, axis=2) - reaching
    is_last = lax.broadcasted_iota(jnp.int32, (length, 1), 0) == length - 1
    cumul_grad = cumul_grad + jnp.where(is_last, end_term[None, :], 0.0)
    decay_grad = jnp.flip(jnp.cumsum(jnp.flip(cumul_grad, 0), axis=0), 0)
    rate_terms = jnp.sum(decay_grad * log_decay, axis=0)
    return grad_input.reshape(length, -1).astype(jnp.bfloat16), grad_inject, grad_read, rate_terms


def reference(cotangent, out_weight, head_input, injector, readout, decay_code, decay_rate, start_state):
    pieces_count = SEQUENCE_LENGTH // S_DEV

    def to_pieces(array):
        return array.reshape((pieces_count, S_DEV) + array.shape[1:])

    def per_sequence(totals, sequence):
        weight_total, rate_total = totals
        grad_out, inputs_seq, inject_seq, read_seq, code_seq, states_seq = sequence
        output_grad = jnp.dot(grad_out, out_weight.T, preferred_element_type=jnp.float32).astype(jnp.bfloat16)
        log_decay = -decay_rate[None, :] * code_seq.astype(jnp.float32)
        pieces = (to_pieces(inputs_seq), to_pieces(inject_seq), to_pieces(read_seq), to_pieces(output_grad), to_pieces(log_decay))
        outputs = lax.map(lambda group: forward_shard(group[0], group[1], group[2], group[4], group[5]), pieces + (states_seq,))
        scales, adjoints = lax.map(lambda group: chain_piece(group[2], group[3], group[4]), pieces)

        def backward_step(incoming, element):
            return element[1] + element[0][:, None, None] * incoming, incoming

        _, incomings = lax.scan(backward_step, jnp.zeros_like(adjoints[0]), (scales, adjoints), reverse=True)
        grad_input, grad_inject, grad_read, rate_terms = lax.map(lambda group: backward_shard(*group), pieces + (states_seq, incomings))
        whole_out = outputs.reshape(SEQUENCE_LENGTH, -1)
        weight_total = weight_total + jnp.dot(whole_out.T, grad_out, preferred_element_type=jnp.float32)
        rate_total = rate_total + jnp.sum(rate_terms, axis=0)
        return (weight_total, rate_total), (grad_input.reshape(SEQUENCE_LENGTH, -1), grad_inject.reshape(SEQUENCE_LENGTH, -1), grad_read.reshape(SEQUENCE_LENGTH, -1))

    initial = (jnp.zeros((H * P_SIZE, D), jnp.float32), jnp.zeros((H,), jnp.float32))
    (weight_total, rate_total), (gradient_input, gradient_injector, gradient_readout) = lax.scan(
        per_sequence, initial, (cotangent, head_input, injector, readout, decay_code, start_state))
    return gradient_input, gradient_injector, gradient_readout, weight_total, rate_total / (SEQUENCE_COUNT * SEQUENCE_LENGTH)
```

```python
import jax
import jax.numpy as jnp
from jax import lax
from jax.experimental import pallas as pl
from jax.experimental.pallas import tpu as pltpu
from jax.sharding import PartitionSpec as P

F32 = jnp.float32
BF16 = jnp.bfloat16
T = 512
D = 8192
HP = 256
N = 128
ROWS = 128
SIDE = 4
DEPTH = 8
VMEM_LIMIT = 48 << 20


def dot(a, b, contract):
    return lax.dot_general(a, b, (contract, ((), ())), preferred_element_type=F32)


def nn(a, b):
    return dot(a, b, ((1,), (0,)))


def nt(a, b):
    return dot(a, b, ((1,), (1,)))


def tn(a, b):
    return dot(a, b, ((0,), (0,)))


def split(a):
    high = a.astype(BF16)
    return high, (a - high.astype(F32)).astype(BF16)


def call(kernel, outs, args, smem=(), flops=0, bytes_accessed=0):
    specs = [
        pl.BlockSpec(memory_space=pltpu.SMEM if i in smem else pltpu.VMEM)
        for i in range(len(args))
    ]
    return pl.pallas_call(
        kernel,
        out_shape=outs,
        in_specs=specs,
        out_specs=jax.tree.map(lambda _: pl.BlockSpec(memory_space=pltpu.VMEM), outs),
        compiler_params=pltpu.CompilerParams(vmem_limit_bytes=VMEM_LIMIT),
        cost_estimate=pl.CostEstimate(
            flops=flops, bytes_accessed=bytes_accessed, transcendentals=0
        ),
    )(*args)


def shape(dims, kind=F32):
    return jax.ShapeDtypeStruct(dims, kind)


def forward_kernel(
    rate_ref, x_ref, inj_ref, rd_ref, code_ref, code_t_ref, state_ref,
    out_t_ref, mix_ref, wts_ref, rate_w_ref, carr_ref, fr_hi_ref, fr_lo_ref, aux_ref,
    chain_ref, decay_ref,
):
    rows = lax.broadcasted_iota(jnp.int32, (T, T), 0)
    cols = lax.broadcasted_iota(jnp.int32, (T, T), 1)
    lower = jnp.where(rows >= cols, 1.0, 0.0).astype(BF16)
    upper = jnp.where(rows <= cols, 1.0, 0.0).astype(BF16)

    def parts(code):
        return (code >> 8).astype(F32).astype(BF16), (code & 255).astype(F32).astype(BF16)

    high, low = parts(code_ref[...])
    count = 256.0 * nn(lower, high) + nn(lower, low)
    high, low = parts(code_t_ref[...])
    count_t = 256.0 * nn(high, upper) + nn(low, upper)
    inject = inj_ref[...]
    read = rd_ref[...]
    inject_f = inject.astype(F32)
    read_f = read.astype(F32)
    lane = lax.broadcasted_iota(jnp.int32, (T, 128), 1)
    aux = jnp.zeros((T, 128), F32)
    decay_rows = []
    for h in range(2):
        rate = rate_ref[h]
        hs = slice(h * 128, h * 128 + 128)
        x = x_ref[:, hs]
        state = state_ref[h]
        s_hi, s_lo = split(state)
        cum = -rate * count[:, h : h + 1]
        cum_end = cum[T - 1 :, :]
        start_w = jnp.exp(cum)
        to_end = jnp.exp(-rate * (count[T - 1 :, h : h + 1] - count[:, h : h + 1]))
        aux = jnp.where(lane == h, to_end, aux)
        aux = jnp.where(lane == 2 + h, start_w, aux)
        fr_hi, fr_lo = split(start_w * read_f)
        fr_hi_ref[h] = fr_hi
        fr_lo_ref[h] = fr_lo
        carried = (nt(read, s_hi) + nt(read, s_lo)) * start_w
        carr_ref[:, hs] = carried * cum
        scaled = (cum_end - cum) * to_end * inject_f
        b_hi, b_lo = split(scaled)
        end_w = jnp.exp(cum_end)
        chain = tn(x, b_hi) + tn(x, b_lo) + (cum_end * end_w) * state
        for z in range(DEPTH):
            chain_ref[z, h * 16 : h * 16 + 16, :] = chain[z * 16 : z * 16 + 16, :]
        decay_rows.append(jnp.broadcast_to(end_w, (1, 128)))
        for i in range(T // ROWS):
            rs = slice(i * ROWS, i * ROWS + ROWS)
            width = (i + 1) * ROWS
            inter = nt(read[rs], inject[:width])
            spread = -rate * (count[rs, h : h + 1] - count_t[h : h + 1, :width])
            keep = rows[rs, :width] >= cols[rs, :width]
            spread = jnp.where(keep, spread, 0.0)
            wts = jnp.where(keep, jnp.exp(spread), 0.0)
            mixed = inter * wts
            narrow = mixed.astype(BF16)
            wts_ref[h, rs, :width] = wts
            rate_w_ref[h, rs, :width] = mixed * spread
            mix_ref[h, rs, :width] = narrow
            within = nn(narrow, x[:width])
            out = within + carried[rs]
            out_t_ref[hs, rs] = out.T.astype(BF16)
    aux_ref[...] = aux
    decay_ref[...] = jnp.concatenate(decay_rows + [jnp.zeros((6, 128), F32)], axis=0)


def weight_send_kernel(pos_ref, out_t_ref, c0, c1, c2, c3, o_ref):
    for dy, c_ref in enumerate((c0, c1, c2, c3)):
        o_ref[0, dy] = nn(out_t_ref[...], c_ref[...]).astype(BF16)


def weight_keep_kernel(pos_ref, out_t_ref, c0, c1, c2, c3, recv_ref, *outs):
    first, second = outs[:SIDE], outs[SIDE:]
    dx = pl.program_id(0)
    for dy, c_ref in enumerate((c0, c1, c2, c3)):
        total = nn(out_t_ref[...], c_ref[...]) + recv_ref[0, dy].astype(F32)
        total = total.astype(BF16)
        second[dy][dx] = total[128:]
        for k in range(SIDE):

            @pl.when(dx == k)
            def _(k=k, dy=dy, total=total):
                first[k][dy] = total[:128]


def weight_terms(pos, out_t, cotangent, recv=None):
    def column(dy):
        def index(dx, pos):
            block = lax.rem(pos[0] + dx, SIDE) * 8 + lax.rem(pos[1] + dy, SIDE) * 2
            return (0, block + (pos[2] if recv is not None else 1 - pos[2]))

        return pl.BlockSpec((T, 256), index)

    in_specs = [pl.BlockSpec((HP, T), lambda dx, pos: (0, 0))]
    in_specs += [column(dy) for dy in range(SIDE)]
    args = [out_t] + [cotangent] * SIDE
    if recv is None:
        kernel = weight_send_kernel
        outs = shape((SIDE, SIDE, 256, 256), BF16)
        out_specs = pl.BlockSpec((1, SIDE, 256, 256), lambda dx, pos: (dx, 0, 0, 0))
    else:
        kernel = weight_keep_kernel
        in_specs.append(pl.BlockSpec((1, SIDE, 256, 256), lambda dx, pos: (dx, 0, 0, 0)))
        args.append(recv)
        outs = [shape((SIDE, 128, 256), BF16)] * (2 * SIDE)
        out_specs = [pl.BlockSpec((SIDE, 128, 256), lambda dx, pos: (0, 0, 0))] * (2 * SIDE)
    return pl.pallas_call(
        kernel,
        out_shape=outs,
        grid_spec=pltpu.PrefetchScalarGridSpec(
            num_scalar_prefetch=1, grid=(SIDE,), in_specs=in_specs, out_specs=out_specs
        ),
        compiler_params=pltpu.CompilerParams(vmem_limit_bytes=VMEM_LIMIT),
        cost_estimate=pl.CostEstimate(
            flops=T * D * HP, bytes_accessed=7 << 20, transcendentals=0
        ),
    )(pos, *args)


def plane_sum_kernel(*refs):
    ins, outs = refs[:8], refs[8:]
    for part in range(2):
        for k in range(SIDE):
            total = ins[part * 4][k].astype(F32)
            for j in range(1, SIDE):
                total = total + ins[part * 4 + j][k].astype(F32)
            outs[part * 4 + k][...] = total


def line_sum_kernel(*refs):
    ins, out_ref = refs[:8], refs[8]
    for part in range(2):
        total = ins[part * 4][...] + ins[part * 4 + 1][...]
        total = total + ins[part * 4 + 2][...] + ins[part * 4 + 3][...]
        for k in range(4):
            out_ref[part * 4 + k] = total[k * 32 : k * 32 + 32, :]


def depth_sum_kernel(in_ref, out_ref):
    total = in_ref[0]
    for k in range(1, DEPTH):
        total = total + in_ref[k]
    out_ref[...] = total


def grad_first_kernel(pos_ref, cot_ref, w_ref, o_ref):
    part = nt(cot_ref[...], w_ref[0])

    @pl.when(pl.program_id(0) == 0)
    def _():
        o_ref[...] = part

    @pl.when(pl.program_id(0) > 0)
    def _():
        o_ref[...] += part


def grad_second_kernel(
    pos_ref, cot_ref, w_ref, first_ref, fr_hi_ref, fr_lo_ref, chain_ref, decay_ref,
    og_ref, pay_ref, acc_ref,
):
    part = nt(cot_ref[...], w_ref[0])
    step = pl.program_id(0)

    @pl.when(step == 0)
    def _():
        acc_ref[...] = part + first_ref[...]

    @pl.when(step > 0)
    def _():
        acc_ref[...] += part

    @pl.when(step == pl.num_programs(0) - 1)
    def _():
        grad = acc_ref[...].astype(BF16)
        og_ref[...] = grad
        for h in range(2):
            g = grad[:, h * 128 : h * 128 + 128]
            adjoint = tn(g, fr_hi_ref[h]) + tn(g, fr_lo_ref[h])
            for z in range(DEPTH):
                pay_ref[z, h * 16 : h * 16 + 16, :] = adjoint[z * 16 : z * 16 + 16, :]
        for z in range(DEPTH):
            pay_ref[z, 32:64, :] = chain_ref[z]
            pay_ref[z, 64:72, :] = decay_ref[...]


def output_grad_part(pos, cotangent, weights, mine, more=None):
    def fixed(dims):
        return pl.BlockSpec(dims, lambda z, pos: (0,) * len(dims))

    in_specs = [
        pl.BlockSpec((T, 512), lambda z, pos: (0, 2 * z + (pos[2] if mine else 1 - pos[2]))),
        pl.BlockSpec((1, HP, 512), lambda z, pos: (z, 0, 0)),
    ]
    scratch = []
    if more is None:
        kernel, outs, out_specs, more = grad_first_kernel, shape((T, HP)), fixed((T, HP)), ()
    else:
        kernel = grad_second_kernel
        in_specs += [fixed(a.shape) for a in more]
        outs = [shape((T, HP), BF16), shape((DEPTH, 72, 128))]
        out_specs = [fixed((T, HP)), fixed((DEPTH, 72, 128))]
        scratch = [pltpu.VMEM((T, HP), F32)]
    return pl.pallas_call(
        kernel,
        out_shape=outs,
        grid_spec=pltpu.PrefetchScalarGridSpec(
            num_scalar_prefetch=1,
            grid=(DEPTH,),
            in_specs=in_specs,
            out_specs=out_specs,
            scratch_shapes=scratch,
        ),
        compiler_params=pltpu.CompilerParams(vmem_limit_bytes=VMEM_LIMIT),
        cost_estimate=pl.CostEstimate(
            flops=T * D * HP, bytes_accessed=7 << 20, transcendentals=0
        ),
    )(pos, cotangent, weights, *more)


def backward_kernel(
    g_ref, x_ref, inj_ref, rd_ref, state_ref, mix_ref, wts_ref, rate_w_ref, carr_ref, aux_ref,
    gi_ref, ginj_ref, gread_ref, rate_ref,
):
    inject = inj_ref[...]
    read = rd_ref[...]
    gi_ref[...] = jnp.zeros((T, HP), F32)
    ginj_ref[...] = jnp.zeros((T, N), F32)
    rate_rows = []
    for h in range(2):
        hs = slice(h * 128, h * 128 + 128)
        x = x_ref[:, hs]
        g = g_ref[:, hs]
        state = state_ref[h].astype(BF16)
        rate = jnp.sum(g.astype(F32) * carr_ref[:, hs], axis=0, keepdims=True)
        for i in range(T // ROWS):
            rs = slice(i * ROWS, i * ROWS + ROWS)
            width = (i + 1) * ROWS
            pairing = nt(g[rs], x[:width])
            rated = jnp.sum(pairing * rate_w_ref[h, rs, :width], axis=0, keepdims=True)
            for j in range(i + 1):
                rate = rate + rated[:, j * ROWS : j * ROWS + ROWS]
            pairing = (pairing * wts_ref[h, rs, :width]).astype(BF16)
            through = nn(g[rs], state) * aux_ref[rs, 2 + h : 3 + h]
            read_part = nn(pairing, inject[:width]) + through
            if h == 0:
                gread_ref[rs, :] = read_part
            else:
                gread_ref[rs, :] += read_part
            ginj_ref[:width, :] += tn(pairing, read[rs])
            gi_ref[:width, hs] += tn(mix_ref[h, rs, :width], g[rs])
        rate_rows.append(rate)
    rate_ref[...] = jnp.concatenate(rate_rows + [jnp.zeros((6, 128), F32)], axis=0)


def scan_kernel(pay_ref, local_ref, inc_ref, rate_ref):
    rates = [local_ref[h : h + 1, :] for h in range(2)]
    for h in range(2):
        hs = slice(h * 16, h * 16 + 16)
        running = jnp.zeros((16, 128), F32)
        for c in range(DEPTH - 1, -1, -1):
            inc_ref[c, hs, :] = running
            rates[h] = rates[h] + jnp.sum(
                running * pay_ref[c, 32 + h * 16 : 48 + h * 16, :], axis=0, keepdims=True
            )
            running = pay_ref[c, hs, :] + pay_ref[c, 64 + h : 65 + h, :] * running
    sums = [jnp.broadcast_to(jnp.sum(r, axis=1, keepdims=True), (1, 128)) for r in rates]
    rate_ref[...] = jnp.concatenate(sums + [jnp.zeros((6, 128), F32)], axis=0)


def finish_kernel(gi_ref, ginj_ref, x_ref, inj_ref, aux_ref, inc_ref, o_gi_ref, o_ginj_ref):
    total = ginj_ref[...]
    inject = inj_ref[...]
    for h in range(2):
        hs = slice(h * 128, h * 128 + 128)
        pieces = [inc_ref[z, h * 16 : h * 16 + 16, :] for z in range(DEPTH)]
        incoming = jnp.concatenate(pieces, axis=0).astype(BF16)
        to_end = aux_ref[:, h : h + 1]
        o_gi_ref[:, hs] = (gi_ref[:, hs] + to_end * nt(inject, incoming)).astype(BF16)
        total = total + to_end * nn(x_ref[:, hs], incoming)
    o_ginj_ref[...] = total


def dp_index(x, y, core):
    return ((x % SIDE) * SIDE + y % SIDE) * 2 + core


def shifts(dx, dy):
    places = [(x, y, c) for x in range(SIDE) for y in range(SIDE) for c in range(2)]
    return [(dp_index(x, y, c), dp_index(x + dx, y + dy, c)) for x, y, c in places]


def flips(bits):
    return [(i, i ^ bits) for i in range(2 * SIDE * SIDE)]


def local(
    cotangent, out_weight, head_input, injector, readout, decay_code, decay_rate, start_state
):
    cot = cotangent[0]
    x = head_input[0]
    inject = injector[0]
    read = readout[0]
    state = start_state[0, 0]
    code = decay_code[0]
    me = lax.axis_index("dp")
    core = me % 2
    pos = jnp.stack([me // 8, (me // 2) % SIDE, core]).astype(jnp.int32)

    half = lax.dynamic_slice_in_dim(out_weight, core * 512, 512, 1)
    mine = lax.all_gather(half, "ctx", axis=0)
    other = lax.ppermute(mine, "dp", flips(1))

    code_cols = jnp.pad(code, ((0, 0), (0, 126)))
    code_rows = jnp.pad(code.T, ((0, 6), (0, 0)))
    out_t, mix, wts, rate_w, carr, fr_hi, fr_lo, aux, chain, decay = call(
        forward_kernel,
        [
            shape((HP, T), BF16), shape((2, T, T), BF16), shape((2, T, T)), shape((2, T, T)),
            shape((T, HP)), shape((2, T, N), BF16), shape((2, T, N), BF16), shape((T, 128)),
            shape((DEPTH, 32, 128)), shape((8, 128)),
        ],
        (decay_rate, x, inject, read, code_cols, code_rows, state),
        smem=(0,), flops=1 << 30, bytes_accessed=8 << 20,
    )

    sent = lax.ppermute(weight_terms(pos, out_t, cot), "dp", flips(1))
    parts = weight_terms(pos, out_t, cot, sent)
    first, second = parts[:SIDE], parts[SIDE:]
    first = [first[0]] + [lax.ppermute(first[d], "dp", shifts(d, 0)) for d in range(1, SIDE)]
    second = [second[0]] + [lax.ppermute(second[d], "dp", shifts(0, d)) for d in range(1, SIDE)]
    parts = call(plane_sum_kernel, [shape((128, 256))] * 8, (*first, *second),
                 flops=4 << 20, bytes_accessed=3 << 20)
    first, second = parts[:SIDE], parts[SIDE:]
    first = [first[0]] + [lax.ppermute(first[d], "dp", shifts(0, d)) for d in range(1, SIDE)]
    second = [second[0]] + [lax.ppermute(second[d], "dp", shifts(d, 0)) for d in range(1, SIDE)]
    blocks = call(line_sum_kernel, shape((DEPTH, 32, 256)), (*first, *second),
                  flops=1 << 20, bytes_accessed=1 << 20)
    blocks = lax.all_to_all(blocks, "ctx", 0, 0, tiled=True)
    grad_weight = call(depth_sum_kernel, shape((32, 256)), (blocks,),
                       flops=1 << 18, bytes_accessed=1 << 18)

    part = output_grad_part(pos, cot, mine, True)
    grad, pay = output_grad_part(pos, cot, other, False, (part, fr_hi, fr_lo, chain, decay))
    pay = lax.all_to_all(pay, "ctx", 0, 0, tiled=True)
    gi, ginj, grad_read, rate_local = call(
        backward_kernel,
        [shape((T, HP)), shape((T, N)), shape((T, N)), shape((8, 128))],
        (grad, x, inject, read, state, mix, wts, rate_w, carr, aux),
        flops=1 << 30, bytes_accessed=8 << 20,
    )
    incoming, rate = call(
        scan_kernel, [shape((DEPTH, 32, 128)), shape((8, 128))], (pay, rate_local),
        flops=1 << 18, bytes_accessed=1 << 19,
    )
    incoming = lax.all_to_all(incoming, "ctx", 0, 0, tiled=True)
    grad_input, grad_inject = call(
        finish_kernel, [shape((T, HP), BF16), shape((T, N))],
        (gi, ginj, x, inject, aux, incoming), flops=1 << 26, bytes_accessed=2 << 20,
    )

    rate = rate + lax.ppermute(rate, "dp", flips(1))
    for unit in (2, 8):
        one, two, three = (lax.ppermute(rate, "dp", flips(unit * k)) for k in (1, 2, 3))
        rate = (rate + two) + (one + three)
    rate = lax.all_to_all(jnp.broadcast_to(rate, (DEPTH, 8, 128)), "ctx", 0, 0, tiled=True)
    rate = jnp.sum(rate[:, :2, 0], axis=0)
    tokens = T * lax.axis_size("dp") * lax.axis_size("ctx")
    return grad_input[None], grad_inject[None], grad_read[None], grad_weight, rate / tokens


def solution(mesh):
    in_specs = (
        P("dp", "ctx", None),
        P(None, "ctx"),
        P("dp", "ctx", None),
        P("dp", "ctx", None),
        P("dp", "ctx", None),
        P("dp", "ctx", None),
        P(),
        P("dp", "ctx", None, None, None),
    )
    out_specs = (
        P("dp", "ctx", None),
        P("dp", "ctx", None),
        P("dp", "ctx", None),
        P("ctx", "dp"),
        P(),
    )
    return jax.shard_map(local, mesh=mesh, in_specs=in_specs, out_specs=out_specs, check_vma=False)
```

```python
import functools

import jax
import jax.numpy as jnp
from jax import lax
from jax.experimental import pallas as pl
from jax.experimental.pallas import tpu as pltpu
from jax.sharding import PartitionSpec as P

F32 = jnp.float32
BF16 = jnp.bfloat16
T = 512
D = 8192
HP = 256
N = 128
ROWS = 128
PLANE = 16
DEPTH = 8
VMEM_LIMIT = 60 << 20


def dot(a, b, contract):
    return lax.dot_general(a, b, (contract, ((), ())), preferred_element_type=F32)


def nn(a, b):
    return dot(a, b, ((1,), (0,)))


def nt(a, b):
    return dot(a, b, ((1,), (1,)))


def tn(a, b):
    return dot(a, b, ((0,), (0,)))


def split(a):
    high = a.astype(BF16)
    return high, (a - high.astype(F32)).astype(BF16)


def call(kernel, outs, args, smem=(), hbm=(), scratch=(), flops=0, bytes_accessed=0):
    def whole(dims):
        return pl.BlockSpec(dims, lambda _: (0,) * len(dims))

    def spec(i, arg):
        if i in smem:
            return pl.BlockSpec(memory_space=pltpu.SMEM)
        return pl.BlockSpec(memory_space=pl.ANY) if i in hbm else whole(arg.shape)

    return pl.pallas_call(
        kernel,
        grid=(1,),
        out_shape=outs,
        in_specs=[spec(i, arg) for i, arg in enumerate(args)],
        out_specs=jax.tree.map(lambda out: whole(out.shape), outs),
        scratch_shapes=scratch,
        compiler_params=pltpu.CompilerParams(vmem_limit_bytes=VMEM_LIMIT),
        cost_estimate=pl.CostEstimate(
            flops=flops, bytes_accessed=bytes_accessed, transcendentals=0
        ),
    )(*args)


def shape(dims, kind=F32):
    return jax.ShapeDtypeStruct(dims, kind)


def counts(code):
    rows = lax.broadcasted_iota(jnp.int32, (T, T), 0)
    cols = lax.broadcasted_iota(jnp.int32, (T, T), 1)
    lower = jnp.where(rows >= cols, 1.0, 0.0).astype(BF16)
    pad = jnp.zeros((126, T), F32)
    high = jnp.concatenate([(code >> 8).astype(F32), pad], axis=0).astype(BF16)
    low = jnp.concatenate([(code & 255).astype(F32), pad], axis=0).astype(BF16)
    return lower, high, low, 256.0 * nt(lower, high) + nt(lower, low)


def payload_kernel(place_ref, rate_ref, half_ref, x_ref, inj_ref, code_ref, state_ref, pay_ref, chain_ref):
    pay_ref[:HP, :] = half_ref[...]
    count = counts(code_ref[...])[3]
    inject_f = inj_ref[...].astype(F32)
    for h in range(2):
        rate = rate_ref[h]
        x = x_ref[:, h * 128 : h * 128 + 128]
        end = count[T - 1 :, h : h + 1]
        span = -rate * (end - count[:, h : h + 1])
        b_hi, b_lo = split(span * jnp.exp(span) * inject_f)
        cum_end = -rate * end
        end_w = jnp.exp(cum_end)
        chain = tn(x, b_hi) + tn(x, b_lo) + (cum_end * end_w) * state_ref[h]
        chain_ref[h, :N, :] = chain
        chain_ref[h, N:, :] = jnp.broadcast_to(end_w, (8, 128))
        for k, term in enumerate(split(chain_ref[h])):
            at = (2 * k + h) * 128
            pay_ref[HP : HP + N + 8, at : at + 128] = term


def forward_kernel(
    rate_ref, x_ref, inj_ref, rd_ref, code_ref, state_ref,
    out_t_ref, mix_ref, wts_ref, part_ref, fr_ref, aux_ref,
):
    rows = lax.broadcasted_iota(jnp.int32, (T, T), 0)
    cols = lax.broadcasted_iota(jnp.int32, (T, T), 1)
    lower, high, low, count = counts(code_ref[...])
    upper = jnp.where(rows <= cols, 1.0, 0.0).astype(BF16)
    count_t = 256.0 * nn(high, upper) + nn(low, upper)
    inject = inj_ref[...]
    read = rd_ref[...]
    read_f = read.astype(F32)
    lane = lax.broadcasted_iota(jnp.int32, (T, 128), 1)
    aux = jnp.zeros((T, 128), F32)
    for h in range(2):
        rate = rate_ref[h]
        hs = slice(h * 128, h * 128 + 128)
        x = x_ref[:, hs]
        state = state_ref[h]
        s_hi, s_lo = split(state)
        cum = -rate * count[:, h : h + 1]
        start_w = jnp.exp(cum)
        to_end = jnp.exp(-rate * (count[T - 1 :, h : h + 1] - count[:, h : h + 1]))
        aux = jnp.where(lane == h, to_end, aux)
        aux = jnp.where(lane == 2 + h, start_w, aux)
        fr_ref[h] = (start_w * read_f).astype(BF16)
        carried = (nt(read, s_hi) + nt(read, s_lo)) * start_w
        weighted = carried * cum
        for i in range(T // ROWS):
            rs = slice(i * ROWS, i * ROWS + ROWS)
            width = (i + 1) * ROWS
            inter = nt(read[rs], inject[:width])
            spread = -rate * (count[rs, h : h + 1] - count_t[h : h + 1, :width])
            keep = rows[rs, :width] >= cols[rs, :width]
            spread = jnp.where(keep, spread, 0.0)
            wts = jnp.where(keep, jnp.exp(spread), 0.0)
            mixed = inter * wts
            narrow = mixed.astype(BF16)
            wts_ref[h, rs, :width] = wts
            r_hi, r_lo = split(mixed * spread)
            part_ref[rs, hs] = weighted[rs] + nn(r_hi, x[:width]) + nn(r_lo, x[:width])
            mix_ref[h, rs, :width] = narrow
            within = nn(narrow, x[:width])
            out = within + carried[rs]
            out_t_ref[hs, rs] = out.T.astype(BF16)
    aux_ref[...] = aux


def fetch(source, target, sem):
    copy = pltpu.make_async_copy(source, target, sem)
    copy.start()
    return copy


def weight_kernel(place_ref, out_t_ref, cot_ref, send_ref, keep_ref):
    core = place_ref[0]
    for k in range(4):
        for ref, side in ((send_ref, 1 - core), (keep_ref, core)):
            block = cot_ref[:, pl.ds(pl.multiple_of((2 * k + side) * 256, 256), 256)]
            ref[k] = nn(out_t_ref[...], block).astype(BF16)


def gridded(kernel, steps, in_specs, out_specs, outs, args, scratch=()):
    return pl.pallas_call(
        kernel,
        out_shape=outs,
        grid_spec=pltpu.PrefetchScalarGridSpec(
            num_scalar_prefetch=1,
            grid=(steps,),
            in_specs=in_specs,
            out_specs=out_specs,
            scratch_shapes=scratch,
        ),
        compiler_params=pltpu.CompilerParams(vmem_limit_bytes=VMEM_LIMIT),
        cost_estimate=pl.CostEstimate(flops=0, bytes_accessed=0, transcendentals=0),
    )(*args)


def fixed(dims):
    return pl.BlockSpec(dims, lambda i, place: (0,) * len(dims))


def core_sum_kernel(kept_ref, recv_ref, o_ref):
    o_ref[...] = (kept_ref[...].astype(F32) + recv_ref[...].astype(F32)).astype(BF16)


def plane_sum_kernel(in_ref, rate_ref, out_ref):
    for z in range(DEPTH):
        rs = slice(z * 32, z * 32 + 32)
        total = in_ref[0, rs, :].astype(F32)
        for k in range(1, PLANE):
            total = total + in_ref[k, rs, :].astype(F32)
        out_ref[z, :32, :] = total
        out_ref[z, 32:, :128] = rate_ref[...]
        out_ref[z, 32:, 128:] = rate_ref[...]


def depth_sum_kernel(tokens, in_ref, out_ref, rate_ref):
    total = in_ref[0]
    for k in range(1, DEPTH):
        total = total + in_ref[k]
    out_ref[...] = total[:32]
    rate_ref[...] = total[32:, :128] / tokens


def rate_vector_kernel(place_ref, part_ref, rd_ref, aux_ref, all_ref, o_ref, later_ref):
    for h in range(2):
        hs = slice(h * 128, h * 128 + 128)
        low = slice(256 + h * 128, 384 + h * 128)
        running = jnp.zeros((N, 128), F32)
        for c in range(DEPTH):
            term = all_ref[c, :, hs].astype(F32) + all_ref[c, :, low].astype(F32)
            decay = term[N : N + 1, :]
            later_ref[c, 8 * h : 8 * h + 8, :] = term[N:, :]
            running = jnp.where(c < place_ref[1], term[:N] + decay * running, running)
        q_hi, q_lo = split(running)
        through = nt(rd_ref[...], q_hi) + nt(rd_ref[...], q_lo)
        o_ref[:, hs] = part_ref[:, hs] + aux_ref[:, 2 + h : 3 + h] * through


def output_grad_kernel(place_ref, cot_ref, mine_ref, other_ref, fr_ref, og_ref, pay_ref, acc):
    core = place_ref[0]
    step = pl.program_id(0)
    total = None
    for k in range(2):
        first = cot_ref[:, pl.ds(pl.multiple_of((2 * k + core) * 512, 512), 512)]
        second = cot_ref[:, pl.ds(pl.multiple_of((2 * k + 1 - core) * 512, 512), 512)]
        terms = nt(first, mine_ref[k]) + nt(second, other_ref[k])
        total = terms if total is None else total + terms

    @pl.when(step == 0)
    def _():
        acc[...] = total

    @pl.when(step > 0)
    def _():
        acc[...] += total

    @pl.when(step == pl.num_programs(0) - 1)
    def _():
        grad = acc[...].astype(BF16)
        og_ref[...] = grad
        for h in range(2):
            hs = slice(h * 128, h * 128 + 128)
            narrow = tn(grad[:, hs], fr_ref[h]).astype(BF16)
            for z in range(DEPTH):
                pay_ref[z, hs, :] = narrow


def rate_kernel(og_ref, vec_ref, rate_ref):
    rates = []
    for h in range(2):
        hs = slice(h * 128, h * 128 + 128)
        rate = jnp.sum(og_ref[:, hs].astype(F32) * vec_ref[:, hs], axis=0, keepdims=True)
        rates.append(jnp.broadcast_to(jnp.sum(rate, axis=1, keepdims=True), (1, 128)))
    rate_ref[...] = jnp.concatenate(rates + [jnp.zeros((6, 128), F32)], axis=0)


def backward_kernel(
    g_ref, x_ref, inj_ref, rd_ref, state_ref, mix_ref, wts_ref, aux_ref, gi_ref, ginj_ref,
    gread_ref,
):
    inject = inj_ref[...]
    read = rd_ref[...]
    gi_ref[...] = jnp.zeros((T, HP), F32)
    ginj_ref[...] = jnp.zeros((T, N), F32)
    for h in range(2):
        hs = slice(h * 128, h * 128 + 128)
        x = x_ref[:, hs]
        g = g_ref[:, hs]
        state = state_ref[h].astype(BF16)
        for i in range(T // ROWS):
            rs = slice(i * ROWS, i * ROWS + ROWS)
            width = (i + 1) * ROWS
            pairing = (nt(g[rs], x[:width]) * wts_ref[h, rs, :width]).astype(BF16)
            through = nn(g[rs], state) * aux_ref[rs, 2 + h : 3 + h]
            read_part = nn(pairing, inject[:width]) + through
            if h == 0:
                gread_ref[rs, :] = read_part
            else:
                gread_ref[rs, :] += read_part
            ginj_ref[:width, :] += tn(pairing, read[rs])
            gi_ref[:width, hs] += tn(mix_ref[h, rs, :width], g[rs])


def finish_kernel(
    place_ref, gi_ref, ginj_ref, x_ref, inj_ref, aux_ref, adj_ref, decay_ref, o_gi_ref, o_ginj_ref,
):
    total = ginj_ref[...]
    inject = inj_ref[...]
    for h in range(2):
        hs = slice(h * 128, h * 128 + 128)
        running = jnp.zeros((128, N), F32)
        for c in range(DEPTH - 1, 0, -1):
            decay = decay_ref[c, 8 * h : 8 * h + 1, :]
            later = adj_ref[c, hs, :].astype(F32) + decay * running
            running = jnp.where(c > place_ref[1], later, running)
        incoming = running.astype(BF16)
        to_end = aux_ref[:, h : h + 1]
        o_gi_ref[:, hs] = (gi_ref[:, hs] + to_end * nt(inject, incoming)).astype(BF16)
        total = total + to_end * nn(x_ref[:, hs], incoming)
    o_ginj_ref[...] = total


def swap_cores(value):
    return lax.ppermute(value, "dp", [(i, i ^ 1) for i in range(2 * PLANE)])


def local(
    cotangent, out_weight, head_input, injector, readout, decay_code, decay_rate, start_state
):
    cot = cotangent[0]
    x = head_input[0]
    inject = injector[0]
    read = readout[0]
    state = start_state[0, 0]
    code = decay_code[0]
    core = lax.axis_index("dp") % 2
    place = jnp.stack([core, lax.axis_index("ctx")]).astype(jnp.int32)

    pay, chain = gridded(
        payload_kernel, 1,
        [
            pl.BlockSpec(memory_space=pltpu.SMEM),
            pl.BlockSpec((HP, 512), lambda i, place: (0, place[0])),
            fixed((T, HP)), fixed((T, N)), fixed((2, T)), fixed((2, N, N)),
        ],
        [fixed((HP + N + 8, 512)), fixed((2, N + 8, 128))],
        [shape((HP + N + 8, 512), BF16), shape((2, N + 8, 128))],
        (place, decay_rate, out_weight, x, inject, code.T, state),
    )
    gathered = lax.all_gather(pay, "ctx", axis=0)
    x, _ = lax.optimization_barrier((x, chain))
    out_t, mix, wts, part, from_start, aux = call(
        forward_kernel,
        [
            shape((HP, T), BF16), shape((2, T, T), BF16), shape((2, T, T)), shape((T, HP)),
            shape((2, T, N), BF16), shape((T, 128)),
        ],
        (decay_rate, x, inject, read, code.T, state), smem=(0,),
    )
    half_terms = shape((PLANE, 256, 256), BF16)
    quarter = pl.BlockSpec((4, 256, 256), lambda i, place: (i, 0, 0))
    sent, kept = gridded(
        weight_kernel, 4,
        [fixed((HP, T)), pl.BlockSpec((T, 2048), lambda i, place: (0, i))],
        [quarter, quarter], [half_terms, half_terms], (place, out_t, cot),
    )
    blocks = call(core_sum_kernel, half_terms, (kept, swap_cores(sent)))
    groups = [[2 * k + c for k in range(PLANE)] for c in range(2)]
    swapped = lax.all_to_all(blocks, "dp", 0, 0, tiled=True, axis_index_groups=groups)

    gathered, _ = lax.optimization_barrier((gathered, swapped))
    mine = gathered[:, :HP, :]
    other = swap_cores(mine)
    vector, decay = call(
        rate_vector_kernel, [shape((T, HP)), shape((DEPTH, 16, 128))],
        (place, part, read, aux, gathered[:, HP:, :]), smem=(0,),
    )
    from_start, _ = lax.optimization_barrier((from_start, vector))
    pair = pl.BlockSpec((2, HP, 512), lambda i, place: (i, 0, 0))
    grad, pay = gridded(
        output_grad_kernel, 4,
        [pl.BlockSpec((T, 2048), lambda i, place: (0, i)), pair, pair, fixed((2, T, N))],
        [fixed((T, HP)), fixed((DEPTH, HP, 128))],
        [shape((T, HP), BF16), shape((DEPTH, HP, 128), BF16)],
        (place, cot, mine, other, from_start), [pltpu.VMEM((T, HP), F32)],
    )
    pay = lax.all_to_all(pay, "ctx", 0, 0, tiled=True)
    rate = plane_total(call(rate_kernel, shape((8, 128)), (grad, vector)))
    gi, ginj, grad_read = call(
        backward_kernel, [shape((T, HP)), shape((T, N)), shape((T, N))],
        (grad, x, inject, read, state, mix, wts, aux),
    )
    swapped, _ = lax.optimization_barrier((swapped, gi))
    blocks = call(plane_sum_kernel, shape((DEPTH, 40, 256)), (swapped, rate))
    blocks, _ = lax.optimization_barrier((blocks, pay))
    blocks = lax.all_to_all(blocks, "ctx", 0, 0, tiled=True)
    grad_input, grad_inject = call(
        finish_kernel, [shape((T, HP), BF16), shape((T, N))],
        (place, gi, ginj, x, inject, aux, pay, decay), smem=(0,),
    )
    tokens = T * lax.axis_size("dp") * lax.axis_size("ctx")
    grad_weight, rate = call(
        functools.partial(depth_sum_kernel, tokens), [shape((32, 256)), shape((8, 128))],
        (blocks,),
    )
    return grad_input[None], grad_inject[None], grad_read[None], grad_weight, rate[:2, 0]


def flipped(value, bits):
    return lax.ppermute(value, "dp", [(i, i ^ bits) for i in range(2 * PLANE)])


def plane_total(value):
    value = value + flipped(value, 1)
    for unit in (2, 8):
        one, two, three = (flipped(value, unit * k) for k in (1, 2, 3))
        value = (value + two) + (one + three)
    return value


def solution(mesh):
    in_specs = (
        P("dp", "ctx", None),
        P(None, "ctx"),
        P("dp", "ctx", None),
        P("dp", "ctx", None),
        P("dp", "ctx", None),
        P("dp", "ctx", None),
        P(),
        P("dp", "ctx", None, None, None),
    )
    out_specs = (
        P("dp", "ctx", None),
        P("dp", "ctx", None),
        P("dp", "ctx", None),
        P("ctx", "dp"),
        P(),
    )
    return jax.shard_map(local, mesh=mesh, in_specs=in_specs, out_specs=out_specs, check_vma=False)
```

```python
import functools

import jax
import jax.numpy as jnp
from jax import lax
from jax.experimental import pallas as pl
from jax.experimental.pallas import tpu as pltpu
from jax.sharding import PartitionSpec as P

F32 = jnp.float32
BF16 = jnp.bfloat16
T = 512
D = 8192
HP = 256
N = 128
SIDE = 4
ROWS = 128
PLANE = 16
DEPTH = 8
VMEM_LIMIT = 60 << 20


def dot(a, b, contract):
    return lax.dot_general(a, b, (contract, ((), ())), preferred_element_type=F32)


def nn(a, b):
    return dot(a, b, ((1,), (0,)))


def nt(a, b):
    return dot(a, b, ((1,), (1,)))


def tn(a, b):
    return dot(a, b, ((0,), (0,)))


def split(a):
    high = a.astype(BF16)
    return high, (a - high.astype(F32)).astype(BF16)


def call(kernel, outs, args, smem=(), hbm=(), scratch=(), flops=0, bytes_accessed=0):
    def whole(dims):
        return pl.BlockSpec(dims, lambda _: (0,) * len(dims))

    def spec(i, arg):
        if i in smem:
            return pl.BlockSpec(memory_space=pltpu.SMEM)
        return pl.BlockSpec(memory_space=pl.ANY) if i in hbm else whole(arg.shape)

    return pl.pallas_call(
        kernel,
        grid=(1,),
        out_shape=outs,
        in_specs=[spec(i, arg) for i, arg in enumerate(args)],
        out_specs=jax.tree.map(lambda out: whole(out.shape), outs),
        scratch_shapes=scratch,
        compiler_params=pltpu.CompilerParams(vmem_limit_bytes=VMEM_LIMIT),
        cost_estimate=pl.CostEstimate(
            flops=flops, bytes_accessed=bytes_accessed, transcendentals=0
        ),
    )(*args)


def shape(dims, kind=F32):
    return jax.ShapeDtypeStruct(dims, kind)


def counts(code):
    rows = lax.broadcasted_iota(jnp.int32, (T, T), 0)
    cols = lax.broadcasted_iota(jnp.int32, (T, T), 1)
    lower = jnp.where(rows >= cols, 1.0, 0.0).astype(BF16)
    pad = jnp.zeros((126, T), F32)
    high = jnp.concatenate([(code >> 8).astype(F32), pad], axis=0).astype(BF16)
    low = jnp.concatenate([(code & 255).astype(F32), pad], axis=0).astype(BF16)
    return lower, high, low, 256.0 * nt(lower, high) + nt(lower, low)


def both_counts(code):
    rows = lax.broadcasted_iota(jnp.int32, (T, T), 0)
    cols = lax.broadcasted_iota(jnp.int32, (T, T), 1)
    upper = jnp.where(rows <= cols, 1.0, 0.0).astype(BF16)
    _, high, low, count = counts(code)
    return rows, cols, count, 256.0 * nn(high, upper) + nn(low, upper)


def payload_kernel(place_ref, rate_ref, half_ref, x_ref, inj_ref, code_ref, state_ref, pay_ref, chain_ref):
    pay_ref[:HP, :] = half_ref[...]
    count = counts(code_ref[...])[3]
    inject_f = inj_ref[...].astype(F32)
    for h in range(2):
        rate = rate_ref[h]
        x = x_ref[:, h * 128 : h * 128 + 128]
        end = count[T - 1 :, h : h + 1]
        span = -rate * (end - count[:, h : h + 1])
        b_hi, b_lo = split(span * jnp.exp(span) * inject_f)
        cum_end = -rate * end
        end_w = jnp.exp(cum_end)
        chain = tn(x, b_hi) + tn(x, b_lo) + (cum_end * end_w) * state_ref[h]
        chain_ref[h, :N, :] = chain
        chain_ref[h, N:, :] = jnp.broadcast_to(end_w, (8, 128))
        for k, term in enumerate(split(chain_ref[h])):
            at = (2 * k + h) * 128
            pay_ref[HP : HP + N + 8, at : at + 128] = term


def forward_kernel(rate_ref, x_ref, inj_ref, rd_ref, code_ref, state_ref, out_t_ref, mix_ref):
    rows, cols, count, count_t = both_counts(code_ref[...])
    inject = inj_ref[...]
    read = rd_ref[...]
    for h in range(2):
        rate = rate_ref[h]
        hs = slice(h * 128, h * 128 + 128)
        x = x_ref[:, hs]
        s_hi, s_lo = split(state_ref[h])
        start_w = jnp.exp(-rate * count[:, h : h + 1])
        carried = (nt(read, s_hi) + nt(read, s_lo)) * start_w
        for i in range(T // ROWS):
            rs = slice(i * ROWS, i * ROWS + ROWS)
            width = (i + 1) * ROWS
            inter = nt(read[rs], inject[:width])
            spread = -rate * (count[rs, h : h + 1] - count_t[h : h + 1, :width])
            keep = rows[rs, :width] >= cols[rs, :width]
            wts = jnp.where(keep, jnp.exp(jnp.where(keep, spread, 0.0)), 0.0)
            narrow = (inter * wts).astype(BF16)
            mix_ref[h, rs, :width] = narrow
            out_t_ref[hs, rs] = (nn(narrow, x[:width]) + carried[rs]).T.astype(BF16)


def prepare_kernel(
    rate_ref, x_ref, inj_ref, rd_ref, code_ref, state_ref, wts_ref, part_ref, fr_ref, aux_ref,
):
    rows, cols, count, count_t = both_counts(code_ref[...])
    inject = inj_ref[...]
    read = rd_ref[...]
    read_f = read.astype(F32)
    lane = lax.broadcasted_iota(jnp.int32, (T, 128), 1)
    aux = jnp.zeros((T, 128), F32)
    for h in range(2):
        rate = rate_ref[h]
        hs = slice(h * 128, h * 128 + 128)
        x = x_ref[:, hs]
        s_hi, s_lo = split(state_ref[h])
        cum = -rate * count[:, h : h + 1]
        start_w = jnp.exp(cum)
        to_end = jnp.exp(-rate * (count[T - 1 :, h : h + 1] - count[:, h : h + 1]))
        aux = jnp.where(lane == h, to_end, aux)
        aux = jnp.where(lane == 2 + h, start_w, aux)
        fr_ref[h] = (start_w * read_f).astype(BF16)
        weighted = (nt(read, s_hi) + nt(read, s_lo)) * (start_w * cum)
        for i in range(T // ROWS):
            rs = slice(i * ROWS, i * ROWS + ROWS)
            width = (i + 1) * ROWS
            inter = nt(read[rs], inject[:width])
            spread = -rate * (count[rs, h : h + 1] - count_t[h : h + 1, :width])
            keep = rows[rs, :width] >= cols[rs, :width]
            spread = jnp.where(keep, spread, 0.0)
            wts = jnp.where(keep, jnp.exp(spread), 0.0)
            wts_ref[h, rs, :width] = wts
            r_hi, r_lo = split(inter * wts * spread)
            part_ref[rs, hs] = weighted[rs] + nn(r_hi, x[:width]) + nn(r_lo, x[:width])
    aux_ref[...] = aux


def fetch(source, target, sem):
    copy = pltpu.make_async_copy(source, target, sem)
    copy.start()
    return copy


def weight_kernel(place_ref, out_t_ref, cot_ref, send_ref, keep_ref):
    core = place_ref[0]
    for k in range(4):
        for ref, side in ((send_ref, 1 - core), (keep_ref, core)):
            block = cot_ref[:, pl.ds(pl.multiple_of((2 * k + side) * 256, 256), 256)]
            ref[k] = nn(out_t_ref[...], block).astype(BF16)


def gridded(kernel, steps, in_specs, out_specs, outs, args, scratch=()):
    return pl.pallas_call(
        kernel,
        out_shape=outs,
        grid_spec=pltpu.PrefetchScalarGridSpec(
            num_scalar_prefetch=1,
            grid=(steps,),
            in_specs=in_specs,
            out_specs=out_specs,
            scratch_shapes=scratch,
        ),
        compiler_params=pltpu.CompilerParams(vmem_limit_bytes=VMEM_LIMIT),
        cost_estimate=pl.CostEstimate(flops=0, bytes_accessed=0, transcendentals=0),
    )(*args)


def fixed(dims):
    return pl.BlockSpec(dims, lambda i, place: (0,) * len(dims))


def core_sum_kernel(place_ref, kept_a, recv_a, kept_b, recv_b, *outs):
    rows = (kept_a[0].astype(F32) + recv_a[0].astype(F32)).astype(BF16)
    cols = (kept_b[:, 0].astype(F32) + recv_b[:, 0].astype(F32)).astype(BF16)
    for d in range(SIDE):

        @pl.when(pl.program_id(0) == d)
        def _(d=d):
            outs[d][...] = rows
            outs[SIDE + d][...] = cols


def line_sum_kernel(place_ref, *refs):
    ins, outs = refs[:8], refs[8:]
    for part in range(2):
        mine = place_ref[3 - part]
        for d in range(SIDE):
            at = lax.rem(mine + d, SIDE)
            total = ins[part * 4][at].astype(F32)
            for j in range(1, SIDE):
                total = total + ins[part * 4 + j][at].astype(F32)
            outs[part * 4 + d][...] = total


def plane_sum_kernel(*refs):
    ins, out_ref = refs[:8], refs[8]
    for part in range(2):
        total = ins[part * 4][...] + ins[part * 4 + 1][...]
        total = total + ins[part * 4 + 2][...] + ins[part * 4 + 3][...]
        for k in range(4):
            out_ref[part * 4 + k] = total[k * 32 : k * 32 + 32, :]


def depth_sum_kernel(in_ref, out_ref):
    total = in_ref[0]
    for k in range(1, DEPTH):
        total = total + in_ref[k]
    out_ref[...] = total


def rate_vector_kernel(
    place_ref, part_ref, rd_ref, aux_ref, gathered_ref, o_ref, later_ref, all_ref, sem,
):
    fetch(gathered_ref.at[:, pl.ds(HP, N + 8), :], all_ref, sem).wait()
    for h in range(2):
        hs = slice(h * 128, h * 128 + 128)
        low = slice(256 + h * 128, 384 + h * 128)
        running = jnp.zeros((N, 128), F32)
        for c in range(DEPTH):
            term = all_ref[c, :, hs].astype(F32) + all_ref[c, :, low].astype(F32)
            decay = term[N : N + 1, :]
            later_ref[c, 8 * h : 8 * h + 8, :] = term[N:, :]
            running = jnp.where(c < place_ref[1], term[:N] + decay * running, running)
        q_hi, q_lo = split(running)
        through = nt(rd_ref[...], q_hi) + nt(rd_ref[...], q_lo)
        o_ref[:, hs] = part_ref[:, hs] + aux_ref[:, 2 + h : 3 + h] * through


def output_grad_kernel(
    place_ref, cot_ref, mine_ref, other_ref, fr_ref, vec_ref, og_ref, pay_ref, acc,
):
    core = place_ref[0]
    step = pl.program_id(0)
    total = None
    for k in range(2):
        first = cot_ref[:, pl.ds(pl.multiple_of((2 * k + core) * 512, 512), 512)]
        second = cot_ref[:, pl.ds(pl.multiple_of((2 * k + 1 - core) * 512, 512), 512)]
        terms = nt(first, mine_ref[k]) + nt(second, other_ref[k])
        total = terms if total is None else total + terms

    @pl.when(step == 0)
    def _():
        acc[...] = total

    @pl.when(step > 0)
    def _():
        acc[...] += total

    @pl.when(step == pl.num_programs(0) - 1)
    def _():
        grad = acc[...].astype(BF16)
        og_ref[...] = grad
        tail = []
        for h in range(2):
            hs = slice(h * 128, h * 128 + 128)
            narrow = tn(grad[:, hs], fr_ref[h]).astype(BF16)
            for z in range(DEPTH):
                pay_ref[z, hs, :] = narrow
            rate = jnp.sum(grad[:, hs].astype(F32) * vec_ref[:, hs], axis=0, keepdims=True)
            rest = jnp.broadcast_to(jnp.sum(rate, axis=1, keepdims=True), (8, 128))
            rest_row = lax.broadcasted_iota(jnp.int32, (8, 128), 0)
            terms = jnp.zeros((8, 128), F32)
            for k in range(3):
                term = rest.astype(BF16).astype(F32)
                terms = jnp.where(rest_row == k, term, terms)
                rest = rest - term
            tail.append(terms)
        tail = jnp.concatenate(tail, axis=0).astype(BF16)
        for z in range(DEPTH):
            pay_ref[z, HP:, :] = tail


def backward_kernel(
    g_ref, x_ref, inj_ref, rd_ref, state_ref, mix_ref, wts_ref, aux_ref, gi_ref, ginj_ref,
    gread_ref,
):
    inject = inj_ref[...]
    read = rd_ref[...]
    gi_ref[...] = jnp.zeros((T, HP), F32)
    ginj_ref[...] = jnp.zeros((T, N), F32)
    for h in range(2):
        hs = slice(h * 128, h * 128 + 128)
        x = x_ref[:, hs]
        g = g_ref[:, hs]
        state = state_ref[h].astype(BF16)
        for i in range(T // ROWS):
            rs = slice(i * ROWS, i * ROWS + ROWS)
            width = (i + 1) * ROWS
            pairing = (nt(g[rs], x[:width]) * wts_ref[h, rs, :width]).astype(BF16)
            through = nn(g[rs], state) * aux_ref[rs, 2 + h : 3 + h]
            read_part = nn(pairing, inject[:width]) + through
            if h == 0:
                gread_ref[rs, :] = read_part
            else:
                gread_ref[rs, :] += read_part
            ginj_ref[:width, :] += tn(pairing, read[rs])
            gi_ref[:width, hs] += tn(mix_ref[h, rs, :width], g[rs])


def finish_kernel(
    place_ref, gi_ref, ginj_ref, x_ref, inj_ref, aux_ref, adj_ref, decay_ref, o_gi_ref, o_ginj_ref,
):
    total = ginj_ref[...]
    inject = inj_ref[...]
    for h in range(2):
        hs = slice(h * 128, h * 128 + 128)
        running = jnp.zeros((128, N), F32)
        for c in range(DEPTH - 1, 0, -1):
            decay = decay_ref[c, 8 * h : 8 * h + 1, :]
            later = adj_ref[c, hs, :].astype(F32) + decay * running
            running = jnp.where(c > place_ref[1], later, running)
        incoming = running.astype(BF16)
        to_end = aux_ref[:, h : h + 1]
        o_gi_ref[:, hs] = (gi_ref[:, hs] + to_end * nt(inject, incoming)).astype(BF16)
        total = total + to_end * nn(x_ref[:, hs], incoming)
    o_ginj_ref[...] = total


def swap_cores(value):
    return lax.ppermute(value, "dp", [(i, i ^ 1) for i in range(2 * PLANE)])


def local(
    cotangent, out_weight, head_input, injector, readout, decay_code, decay_rate, start_state
):
    cot = cotangent[0]
    x = head_input[0]
    inject = injector[0]
    read = readout[0]
    state = start_state[0, 0]
    code = decay_code[0]
    core = lax.axis_index("dp") % 2
    me = lax.axis_index("dp")
    place = jnp.stack([core, lax.axis_index("ctx"), me // 8, me // 2 % SIDE]).astype(jnp.int32)

    pay, chain = gridded(
        payload_kernel, 1,
        [
            pl.BlockSpec(memory_space=pltpu.SMEM),
            pl.BlockSpec((HP, 512), lambda i, place: (0, place[0])),
            fixed((T, HP)), fixed((T, N)), fixed((2, T)), fixed((2, N, N)),
        ],
        [fixed((HP + N + 8, 512)), fixed((2, N + 8, 128))],
        [shape((HP + N + 8, 512), BF16), shape((2, N + 8, 128))],
        (place, decay_rate, out_weight, x, inject, code.T, state),
    )
    gathered = lax.all_gather(pay, "ctx", axis=0)
    x, _ = lax.optimization_barrier((x, chain))
    out_t, mix = call(
        forward_kernel, [shape((HP, T), BF16), shape((2, T, T), BF16)],
        (decay_rate, x, inject, read, code.T, state), smem=(0,),
    )
    half_terms = shape((PLANE, 256, 256), BF16)
    part_spec = pl.BlockSpec((4, 256, 256), lambda i, place: (i, 0, 0))
    sent, kept = gridded(
        weight_kernel, 4,
        [fixed((HP, T)), pl.BlockSpec((T, 2048), lambda i, place: (0, i))],
        [part_spec, part_spec], [half_terms, half_terms], (place, out_t, cot),
    )
    parts = core_sum(place, kept, swap_cores(sent))
    first = exchanged(parts[:SIDE], 8)
    second = exchanged(parts[SIDE:], 2)
    parts = call(line_sum_kernel, [shape((128, 256))] * 8, (place, *first, *second), smem=(0,))

    read_later, _ = lax.optimization_barrier((read, kept))
    wts, part, from_start, aux = call(
        prepare_kernel,
        [shape((2, T, T)), shape((T, HP)), shape((2, T, N), BF16), shape((T, 128))],
        (decay_rate, x, inject, read_later, code.T, state), smem=(0,),
    )

    gathered, _ = lax.optimization_barrier((gathered, (parts, aux)))
    mine = gathered[:, :HP, :]
    other = swap_cores(mine)
    vector, decay = call(
        rate_vector_kernel, [shape((T, HP)), shape((DEPTH, 16, 128))],
        (place, part, read, aux, gathered), smem=(0,), hbm=(4,),
        scratch=[pltpu.VMEM((DEPTH, N + 8, 512), BF16), pltpu.SemaphoreType.DMA],
    )
    one = pl.BlockSpec((2, HP, 512), lambda i, place: (i, 0, 0))
    grad, pay = gridded(
        output_grad_kernel, 4,
        [
            pl.BlockSpec((T, 2048), lambda i, place: (0, i)), one, one, fixed((2, T, N)),
            fixed((T, HP)),
        ],
        [fixed((T, HP)), fixed((DEPTH, HP + 16, 128))],
        [shape((T, HP), BF16), shape((DEPTH, HP + 16, 128), BF16)],
        (place, cot, mine, other, from_start, vector), [pltpu.VMEM((T, HP), F32)],
    )
    parts, _ = lax.optimization_barrier((parts, pay))
    first = exchanged(parts[:SIDE], 2)
    second = exchanged(parts[SIDE:], 8)
    pay = lax.all_to_all(pay, "ctx", 0, 0, tiled=True)
    gi, ginj, grad_read = call(
        backward_kernel, [shape((T, HP)), shape((T, N)), shape((T, N))],
        (grad, x, inject, read, state, mix, wts, aux),
    )
    blocks = call(plane_sum_kernel, shape((DEPTH, 32, 256)), (*first, *second))
    blocks, pay = lax.optimization_barrier((blocks, pay))
    blocks = lax.all_to_all(blocks, "ctx", 0, 0, tiled=True)
    rate = jnp.sum(pay[:, HP:, :].astype(F32).reshape(DEPTH, 2, 8, 128), axis=(0, 2))
    rate = plane_total(rate)
    grad_input, grad_inject = call(
        finish_kernel, [shape((T, HP), BF16), shape((T, N))],
        (place, gi, ginj, x, inject, aux, pay, decay), smem=(0,),
    )
    grad_weight = call(depth_sum_kernel, shape((32, 256)), (blocks,))
    tokens = T * lax.axis_size("dp") * lax.axis_size("ctx")
    return grad_input[None], grad_inject[None], grad_read[None], grad_weight, rate[:, 0] / tokens


def core_sum(place, kept, recv):
    kept, recv = (a.reshape(SIDE, SIDE, 256, 256) for a in (kept, recv))
    by_x = pl.BlockSpec(
        (1, SIDE, 128, 256), lambda d, place: (lax.rem(place[2] + d, SIDE), 0, 0, 0)
    )
    by_y = pl.BlockSpec(
        (SIDE, 1, 128, 256), lambda d, place: (0, lax.rem(place[3] + d, SIDE), 1, 0)
    )
    part = (SIDE, 128, 256)
    return gridded(
        core_sum_kernel, SIDE, [by_x, by_x, by_y, by_y], [fixed(part)] * 8,
        [shape(part, BF16)] * 8, (place, kept, recv, kept, recv),
    )


def exchanged(parts, unit):
    def pairs(d):
        def target(i):
            at = i // unit % SIDE
            return i + ((at + d) % SIDE - at) * unit

        return [(i, target(i)) for i in range(2 * PLANE)]

    return [parts[0]] + [lax.ppermute(parts[d], "dp", pairs(d)) for d in range(1, SIDE)]


def flipped(value, bits):
    return lax.ppermute(value, "dp", [(i, i ^ bits) for i in range(2 * PLANE)])


def plane_total(value):
    value = value + flipped(value, 1)
    for unit in (2, 8):
        one, two, three = (flipped(value, unit * k) for k in (1, 2, 3))
        value = (value + two) + (one + three)
    return value


def solution(mesh):
    in_specs = (
        P("dp", "ctx", None),
        P(None, "ctx"),
        P("dp", "ctx", None),
        P("dp", "ctx", None),
        P("dp", "ctx", None),
        P("dp", "ctx", None),
        P(),
        P("dp", "ctx", None, None, None),
    )
    out_specs = (
        P("dp", "ctx", None),
        P("dp", "ctx", None),
        P("dp", "ctx", None),
        P("ctx", "dp"),
        P(),
    )
    return jax.shard_map(local, mesh=mesh, in_specs=in_specs, out_specs=out_specs, check_vma=False)
```

```python
import functools

import jax
import jax.numpy as jnp
from jax import lax
from jax.experimental import pallas as pl
from jax.experimental.pallas import tpu as pltpu
from jax.sharding import PartitionSpec as P

F32 = jnp.float32
BF16 = jnp.bfloat16
T = 512
D = 8192
HP = 256
N = 128
SIDE = 4
WEIGHT_STEPS = 2
ROWS = 128
PLANE = 16
DEPTH = 8
VMEM_LIMIT = 60 << 20


def dot(a, b, contract):
    return lax.dot_general(a, b, (contract, ((), ())), preferred_element_type=F32)


def nn(a, b):
    return dot(a, b, ((1,), (0,)))


def nt(a, b):
    return dot(a, b, ((1,), (1,)))


def tn(a, b):
    return dot(a, b, ((0,), (0,)))


def split(a):
    high = a.astype(BF16)
    return high, (a - high.astype(F32)).astype(BF16)


def call(
    kernel, outs, args, smem=(), hbm=(), scratch=(), limit=VMEM_LIMIT, flops=0, bytes_accessed=0
):
    def whole(dims):
        return pl.BlockSpec(dims, lambda _: (0,) * len(dims))

    def spec(i, arg):
        if i in smem:
            return pl.BlockSpec(memory_space=pltpu.SMEM)
        return pl.BlockSpec(memory_space=pl.ANY) if i in hbm else whole(arg.shape)

    return pl.pallas_call(
        kernel,
        grid=(1,),
        out_shape=outs,
        in_specs=[spec(i, arg) for i, arg in enumerate(args)],
        out_specs=jax.tree.map(lambda out: whole(out.shape), outs),
        scratch_shapes=scratch,
        compiler_params=pltpu.CompilerParams(vmem_limit_bytes=limit),
        cost_estimate=pl.CostEstimate(
            flops=flops, bytes_accessed=bytes_accessed, transcendentals=0
        ),
    )(*args)


def shape(dims, kind=F32):
    return jax.ShapeDtypeStruct(dims, kind)


def counts(code):
    rows = lax.broadcasted_iota(jnp.int32, (T, T), 0)
    cols = lax.broadcasted_iota(jnp.int32, (T, T), 1)
    lower = jnp.where(rows >= cols, 1.0, 0.0).astype(BF16)
    pad = jnp.zeros((126, T), F32)
    high = jnp.concatenate([(code >> 8).astype(F32), pad], axis=0).astype(BF16)
    low = jnp.concatenate([(code & 255).astype(F32), pad], axis=0).astype(BF16)
    return lower, high, low, 256.0 * nt(lower, high) + nt(lower, low)


def both_counts(code):
    rows = lax.broadcasted_iota(jnp.int32, (T, T), 0)
    cols = lax.broadcasted_iota(jnp.int32, (T, T), 1)
    upper = jnp.where(rows <= cols, 1.0, 0.0).astype(BF16)
    _, high, low, count = counts(code)
    return rows, cols, count, 256.0 * nn(high, upper) + nn(low, upper)


def payload_kernel(
    rate_ref, weight_ref, x_ref, inj_ref, code_ref, state_ref, pay_ref, chain_ref, sem,
):
    core = lax.rem(lax.axis_index("dp"), 2)
    half = weight_ref.at[:, pl.ds(pl.multiple_of(core * 512, 512), 512)]
    copy = fetch(half, pay_ref.at[pl.ds(0, HP), :], sem)
    count = counts(code_ref[...])[3]
    inject_f = inj_ref[...].astype(F32)
    for h in range(2):
        rate = rate_ref[h]
        x = x_ref[:, h * 128 : h * 128 + 128]
        end = count[T - 1 :, h : h + 1]
        span = -rate * (end - count[:, h : h + 1])
        b_hi, b_lo = split(span * jnp.exp(span) * inject_f)
        cum_end = -rate * end
        end_w = jnp.exp(cum_end)
        chain = tn(x, b_hi) + tn(x, b_lo) + (cum_end * end_w) * state_ref[h]
        chain_ref[h, :N, :] = chain
        chain_ref[h, N:, :] = jnp.broadcast_to(end_w, (8, 128))
        for k, term in enumerate(split(chain_ref[h])):
            at = (2 * k + h) * 128
            pay_ref[HP : HP + N + 8, at : at + 128] = term
    copy.wait()


def forward_kernel(rate_ref, x_ref, inj_ref, rd_ref, code_ref, state_ref, out_t_ref, mix_ref):
    rows, cols, count, count_t = both_counts(code_ref[...])
    inject = inj_ref[...]
    read = rd_ref[...]
    for h in range(2):
        rate = rate_ref[h]
        hs = slice(h * 128, h * 128 + 128)
        x = x_ref[:, hs]
        s_hi, s_lo = split(state_ref[h])
        start_w = jnp.exp(-rate * count[:, h : h + 1])
        carried = (nt(read, s_hi) + nt(read, s_lo)) * start_w
        for i in range(T // ROWS):
            rs = slice(i * ROWS, i * ROWS + ROWS)
            width = (i + 1) * ROWS
            inter = nt(read[rs], inject[:width])
            spread = -rate * (count[rs, h : h + 1] - count_t[h : h + 1, :width])
            keep = rows[rs, :width] >= cols[rs, :width]
            wts = jnp.where(keep, jnp.exp(jnp.where(keep, spread, 0.0)), 0.0)
            narrow = (inter * wts).astype(BF16)
            mix_ref[h, rs, :width] = narrow
            out_t_ref[hs, rs] = (nn(narrow, x[:width]) + carried[rs]).T.astype(BF16)


def prepare_kernel(
    rate_ref, x_ref, inj_ref, rd_ref, code_ref, state_ref, wts_ref, part_ref, fr_ref, aux_ref,
):
    rows, cols, count, count_t = both_counts(code_ref[...])
    inject = inj_ref[...]
    read = rd_ref[...]
    read_f = read.astype(F32)
    lane = lax.broadcasted_iota(jnp.int32, (T, 128), 1)
    aux = jnp.zeros((T, 128), F32)
    for h in range(2):
        rate = rate_ref[h]
        hs = slice(h * 128, h * 128 + 128)
        x = x_ref[:, hs]
        s_hi, s_lo = split(state_ref[h])
        cum = -rate * count[:, h : h + 1]
        start_w = jnp.exp(cum)
        to_end = jnp.exp(-rate * (count[T - 1 :, h : h + 1] - count[:, h : h + 1]))
        aux = jnp.where(lane == h, to_end, aux)
        aux = jnp.where(lane == 2 + h, start_w, aux)
        fr_ref[h] = (start_w * read_f).astype(BF16)
        weighted = (nt(read, s_hi) + nt(read, s_lo)) * (start_w * cum)
        for i in range(T // ROWS):
            rs = slice(i * ROWS, i * ROWS + ROWS)
            width = (i + 1) * ROWS
            inter = nt(read[rs], inject[:width])
            spread = -rate * (count[rs, h : h + 1] - count_t[h : h + 1, :width])
            keep = rows[rs, :width] >= cols[rs, :width]
            spread = jnp.where(keep, spread, 0.0)
            wts = jnp.where(keep, jnp.exp(spread), 0.0)
            wts_ref[h, rs, :width] = wts.astype(BF16)
            r_hi, r_lo = split(inter * wts * spread)
            part_ref[rs, hs] = weighted[rs] + nn(r_hi, x[:width]) + nn(r_lo, x[:width])
    aux_ref[...] = aux


def fetch(source, target, sem):
    copy = pltpu.make_async_copy(source, target, sem)
    copy.start()
    return copy


def weight_kernel(out_t_ref, cot_ref, send_ref, keep_ref):
    core = lax.rem(lax.axis_index("dp"), 2)
    for k in range(PLANE // WEIGHT_STEPS):
        for ref, side in ((send_ref, 1 - core), (keep_ref, core)):
            block = cot_ref[:, pl.ds(pl.multiple_of((2 * k + side) * 256, 256), 256)]
            ref[k] = nn(out_t_ref[...], block).astype(BF16)


def gridded(kernel, steps, in_specs, out_specs, outs, args, scratch=(), limit=VMEM_LIMIT):
    return pl.pallas_call(
        kernel,
        out_shape=outs,
        grid_spec=pltpu.PrefetchScalarGridSpec(
            num_scalar_prefetch=1,
            grid=(steps,),
            in_specs=in_specs,
            out_specs=out_specs,
            scratch_shapes=scratch,
        ),
        compiler_params=pltpu.CompilerParams(vmem_limit_bytes=limit),
        cost_estimate=pl.CostEstimate(flops=0, bytes_accessed=0, transcendentals=0),
    )(*args)


def fixed(dims):
    return pl.BlockSpec(dims, lambda i, place: (0,) * len(dims))


def core_sum_kernel(place_ref, kept_a, recv_a, kept_b, recv_b, *outs):
    rows = (kept_a[0].astype(F32) + recv_a[0].astype(F32)).astype(BF16)
    cols = (kept_b[:, 0].astype(F32) + recv_b[:, 0].astype(F32)).astype(BF16)
    for d in range(SIDE):

        @pl.when(pl.program_id(0) == d)
        def _(d=d):
            outs[d][...] = rows
            outs[SIDE + d][...] = cols


def line_sum_kernel(place_ref, *refs):
    ins, outs = refs[:8], refs[8:]
    for part in range(2):
        mine = place_ref[3 - part]
        for d in range(SIDE):
            at = lax.rem(mine + d, SIDE)
            total = ins[part * 4][at].astype(F32)
            for j in range(1, SIDE):
                total = total + ins[part * 4 + j][at].astype(F32)
            outs[part * 4 + d][...] = total


def plane_sum_kernel(*refs):
    ins, out_ref = refs[:8], refs[8]
    for part in range(2):
        total = ins[part * 4][...] + ins[part * 4 + 1][...]
        total = total + ins[part * 4 + 2][...] + ins[part * 4 + 3][...]
        for k in range(4):
            out_ref[part * 4 + k] = total[k * 32 : k * 32 + 32, :]


def rate_vector_kernel(
    place_ref, part_ref, rd_ref, aux_ref, gathered_ref, o_ref, later_ref, all_ref, sem,
):
    fetch(gathered_ref.at[:, pl.ds(HP, N + 8), :], all_ref, sem).wait()
    for h in range(2):
        hs = slice(h * 128, h * 128 + 128)
        low = slice(256 + h * 128, 384 + h * 128)
        running = jnp.zeros((N, 128), F32)
        for c in range(DEPTH):
            term = all_ref[c, :, hs].astype(F32) + all_ref[c, :, low].astype(F32)
            decay = term[N : N + 1, :]
            later_ref[c, 8 * h : 8 * h + 8, :] = term[N:, :]
            running = jnp.where(c < place_ref[1], term[:N] + decay * running, running)
        q_hi, q_lo = split(running)
        through = nt(rd_ref[...], q_hi) + nt(rd_ref[...], q_lo)
        o_ref[:, hs] = part_ref[:, hs] + aux_ref[:, 2 + h : 3 + h] * through


def output_grad_kernel(
    place_ref, cot_ref, mine_ref, other_ref, fr_ref, vec_ref, og_ref, pay_ref, acc,
):
    core = place_ref[0]
    step = pl.program_id(0)
    total = None
    for k in range(4):
        first = cot_ref[:, pl.ds(pl.multiple_of((2 * k + core) * 512, 512), 512)]
        second = cot_ref[:, pl.ds(pl.multiple_of((2 * k + 1 - core) * 512, 512), 512)]
        terms = nt(first, mine_ref[k]) + nt(second, other_ref[k])
        total = terms if total is None else total + terms

    @pl.when(step == 0)
    def _():
        acc[...] = total

    @pl.when(step > 0)
    def _():
        acc[...] += total

    @pl.when(step == pl.num_programs(0) - 1)
    def _():
        grad = acc[...].astype(BF16)
        og_ref[...] = grad
        tail = []
        for h in range(2):
            hs = slice(h * 128, h * 128 + 128)
            narrow = tn(grad[:, hs], fr_ref[h]).astype(BF16)
            for z in range(DEPTH):
                pay_ref[z, hs, :] = narrow
            rate = jnp.sum(grad[:, hs].astype(F32) * vec_ref[:, hs], axis=0, keepdims=True)
            rest = jnp.broadcast_to(jnp.sum(rate, axis=1, keepdims=True), (8, 128))
            rest_row = lax.broadcasted_iota(jnp.int32, (8, 128), 0)
            terms = jnp.zeros((8, 128), F32)
            for k in range(3):
                term = rest.astype(BF16).astype(F32)
                terms = jnp.where(rest_row == k, term, terms)
                rest = rest - term
            tail.append(terms)
        tail = jnp.concatenate(tail, axis=0).astype(BF16)
        for z in range(DEPTH):
            pay_ref[z, HP:, :] = tail


def backward_kernel(
    g_ref, x_ref, inj_ref, rd_ref, state_ref, mix_ref, wts_ref, aux_ref, gi_ref, ginj_ref,
    gread_ref,
):
    inject = inj_ref[...]
    read = rd_ref[...]
    gi_ref[...] = jnp.zeros((T, HP), F32)
    ginj_ref[...] = jnp.zeros((T, N), F32)
    for h in range(2):
        hs = slice(h * 128, h * 128 + 128)
        x = x_ref[:, hs]
        g = g_ref[:, hs]
        state = state_ref[h].astype(BF16)
        for i in range(T // ROWS):
            rs = slice(i * ROWS, i * ROWS + ROWS)
            width = (i + 1) * ROWS
            pairing = (nt(g[rs], x[:width]) * wts_ref[h, rs, :width].astype(F32)).astype(BF16)
            through = nn(g[rs], state) * aux_ref[rs, 2 + h : 3 + h]
            read_part = nn(pairing, inject[:width]) + through
            if h == 0:
                gread_ref[rs, :] = read_part
            else:
                gread_ref[rs, :] += read_part
            ginj_ref[:width, :] += tn(pairing, read[rs])
            gi_ref[:width, hs] += tn(mix_ref[h, rs, :width], g[rs])


def finish_kernel(
    place_ref, gi_ref, ginj_ref, x_ref, inj_ref, aux_ref, adj_ref, decay_ref, o_gi_ref, o_ginj_ref,
):
    total = ginj_ref[...]
    inject = inj_ref[...]
    for h in range(2):
        hs = slice(h * 128, h * 128 + 128)
        running = jnp.zeros((128, N), F32)
        for c in range(DEPTH - 1, 0, -1):
            decay = decay_ref[c, 8 * h : 8 * h + 1, :]
            later = adj_ref[c, hs, :].astype(F32) + decay * running
            running = jnp.where(c > place_ref[1], later, running)
        incoming = running.astype(BF16)
        to_end = aux_ref[:, h : h + 1]
        o_gi_ref[:, hs] = (gi_ref[:, hs] + to_end * nt(inject, incoming)).astype(BF16)
        total = total + to_end * nn(x_ref[:, hs], incoming)
    o_ginj_ref[...] = total


def swap_cores(value):
    return lax.ppermute(value, "dp", [(i, i ^ 1) for i in range(2 * PLANE)])


def local(
    cotangent, out_weight, head_input, injector, readout, decay_code, decay_rate, start_state
):
    cot = cotangent[0]
    x = head_input[0]
    inject = injector[0]
    read = readout[0]
    state = start_state[0, 0]
    code = decay_code[0]
    core = lax.axis_index("dp") % 2
    me = lax.axis_index("dp")
    place = jnp.stack([core, lax.axis_index("ctx"), me // 8, me // 2 % SIDE]).astype(jnp.int32)

    pay, chain = call(
        payload_kernel, [shape((HP + N + 8, 512), BF16), shape((2, N + 8, 128))],
        (decay_rate, out_weight, x, inject, code.T, state), smem=(0,), hbm=(1,),
        scratch=[pltpu.SemaphoreType.DMA],
    )
    gathered = lax.all_gather(pay, "ctx", axis=0)
    x, _ = lax.optimization_barrier((x, chain))
    out_t, mix = call(
        forward_kernel, [shape((HP, T), BF16), shape((2, T, T), BF16)],
        (decay_rate, x, inject, read, code.T, state), smem=(0,),
    )
    half_terms = shape((PLANE, 256, 256), BF16)
    width = D // WEIGHT_STEPS
    part_spec = pl.BlockSpec((PLANE // WEIGHT_STEPS, 256, 256), lambda i: (i, 0, 0))
    sent, kept = pl.pallas_call(
        weight_kernel,
        grid=(WEIGHT_STEPS,),
        out_shape=[half_terms, half_terms],
        in_specs=[
            pl.BlockSpec((HP, T), lambda i: (0, 0)),
            pl.BlockSpec((T, width), lambda i: (0, i)),
        ],
        out_specs=[part_spec, part_spec],
        compiler_params=pltpu.CompilerParams(vmem_limit_bytes=VMEM_LIMIT),
        cost_estimate=pl.CostEstimate(flops=0, bytes_accessed=0, transcendentals=0),
    )(out_t, cot)
    parts = core_sum(place, kept, swap_cores(sent))
    first = exchanged(parts[:SIDE], 8)
    second = exchanged(parts[SIDE:], 2)
    parts = call(line_sum_kernel, [shape((128, 256))] * 8, (place, *first, *second), smem=(0,), limit=16 << 20)

    read_later, _ = lax.optimization_barrier((read, kept))
    wts, part, from_start, aux = call(
        prepare_kernel,
        [shape((2, T, T), BF16), shape((T, HP)), shape((2, T, N), BF16), shape((T, 128))],
        (decay_rate, x, inject, read_later, code.T, state), smem=(0,),
    )

    gathered, _ = lax.optimization_barrier((gathered, (parts, aux)))
    mine = gathered[:, :HP, :]
    other = swap_cores(mine)
    vector, decay = call(
        rate_vector_kernel, [shape((T, HP)), shape((DEPTH, 16, 128))],
        (place, part, read, aux, gathered), smem=(0,), hbm=(4,),
        scratch=[pltpu.VMEM((DEPTH, N + 8, 512), BF16), pltpu.SemaphoreType.DMA],
    )
    one = pl.BlockSpec((4, HP, 512), lambda i, place: (i, 0, 0))
    grad, pay = gridded(
        output_grad_kernel, 2,
        [
            pl.BlockSpec((T, 4096), lambda i, place: (0, i)), one, one, fixed((2, T, N)),
            fixed((T, HP)),
        ],
        [fixed((T, HP)), fixed((DEPTH, HP + 16, 128))],
        [shape((T, HP), BF16), shape((DEPTH, HP + 16, 128), BF16)],
        (place, cot, mine, other, from_start, vector), [pltpu.VMEM((T, HP), F32)],
    )
    parts, _ = lax.optimization_barrier((parts, pay))
    first = exchanged(parts[:SIDE], 2)
    second = exchanged(parts[SIDE:], 8)
    pay = lax.all_to_all(pay, "ctx", 0, 0, tiled=True)
    gi, ginj, grad_read = call(
        backward_kernel, [shape((T, HP)), shape((T, N)), shape((T, N))],
        (grad, x, inject, read, state, mix, wts, aux),
    )
    first[1:], _ = lax.optimization_barrier((first[1:], gi))
    blocks = call(plane_sum_kernel, shape((DEPTH, 32, 256)), (*first, *second), limit=16 << 20)
    blocks, pay = lax.optimization_barrier((blocks, pay))
    blocks = lax.all_to_all(blocks, "ctx", 0, 0, tiled=True)
    rate = jnp.sum(pay[:, HP:, :].astype(F32).reshape(DEPTH, 2, 8, 128), axis=(0, 2))
    rate = plane_total(rate)
    grad_input, grad_inject = call(
        finish_kernel, [shape((T, HP), BF16), shape((T, N))],
        (place, gi, ginj, x, inject, aux, pay, decay), smem=(0,),
    )
    grad_weight = jnp.sum(blocks, axis=0)
    tokens = T * lax.axis_size("dp") * lax.axis_size("ctx")
    return grad_input[None], grad_inject[None], grad_read[None], grad_weight, rate[:, 0] / tokens


def core_sum(place, kept, recv):
    kept, recv = (a.reshape(SIDE, SIDE, 256, 256) for a in (kept, recv))
    by_x = pl.BlockSpec(
        (1, SIDE, 128, 256), lambda d, place: (lax.rem(place[2] + d, SIDE), 0, 0, 0)
    )
    by_y = pl.BlockSpec(
        (SIDE, 1, 128, 256), lambda d, place: (0, lax.rem(place[3] + d, SIDE), 1, 0)
    )
    part = (SIDE, 128, 256)
    return gridded(
        core_sum_kernel, SIDE, [by_x, by_x, by_y, by_y], [fixed(part)] * 8,
        [shape(part, BF16)] * 8, (place, kept, recv, kept, recv), limit=16 << 20,
    )


def exchanged(parts, unit):
    def pairs(d):
        def target(i):
            at = i // unit % SIDE
            return i + ((at + d) % SIDE - at) * unit

        return [(i, target(i)) for i in range(2 * PLANE)]

    return [parts[0]] + [lax.ppermute(parts[d], "dp", pairs(d)) for d in range(1, SIDE)]


def flipped(value, bits):
    return lax.ppermute(value, "dp", [(i, i ^ bits) for i in range(2 * PLANE)])


def plane_total(value):
    value = value + flipped(value, 1)
    for unit in (2, 8):
        one, two, three = (flipped(value, unit * k) for k in (1, 2, 3))
        value = (value + two) + (one + three)
    return value


def solution(mesh):
    in_specs = (
        P("dp", "ctx", None),
        P(None, "ctx"),
        P("dp", "ctx", None),
        P("dp", "ctx", None),
        P("dp", "ctx", None),
        P("dp", "ctx", None),
        P(),
        P("dp", "ctx", None, None, None),
    )
    out_specs = (
        P("dp", "ctx", None),
        P("dp", "ctx", None),
        P("dp", "ctx", None),
        P("ctx", "dp"),
        P(),
    )
    return jax.shard_map(local, mesh=mesh, in_specs=in_specs, out_specs=out_specs, check_vma=False)
```

```python
import functools

import jax
import jax.numpy as jnp
from jax import lax
from jax.experimental import pallas as pl
from jax.experimental.pallas import tpu as pltpu
from jax.sharding import PartitionSpec as P

F32 = jnp.float32
BF16 = jnp.bfloat16
T = 512
D = 8192
HP = 256
N = 128
SIDE = 4
WEIGHT_STEPS = 2
ROWS = 128
PLANE = 16
DEPTH = 8
VMEM_LIMIT = 60 << 20


def dot(a, b, contract):
    return lax.dot_general(a, b, (contract, ((), ())), preferred_element_type=F32)


def nn(a, b):
    return dot(a, b, ((1,), (0,)))


def nt(a, b):
    return dot(a, b, ((1,), (1,)))


def tn(a, b):
    return dot(a, b, ((0,), (0,)))


def split(a):
    high = a.astype(BF16)
    return high, (a - high.astype(F32)).astype(BF16)


def call(
    kernel, outs, args, smem=(), hbm=(), scratch=(), limit=VMEM_LIMIT, flops=0, bytes_accessed=0
):
    def whole(dims):
        return pl.BlockSpec(dims, lambda _: (0,) * len(dims))

    def spec(i, arg):
        if i in smem:
            return pl.BlockSpec(memory_space=pltpu.SMEM)
        return pl.BlockSpec(memory_space=pl.ANY) if i in hbm else whole(arg.shape)

    return pl.pallas_call(
        kernel,
        grid=(1,),
        out_shape=outs,
        in_specs=[spec(i, arg) for i, arg in enumerate(args)],
        out_specs=jax.tree.map(lambda out: whole(out.shape), outs),
        scratch_shapes=scratch,
        compiler_params=pltpu.CompilerParams(vmem_limit_bytes=limit),
        cost_estimate=pl.CostEstimate(
            flops=flops, bytes_accessed=bytes_accessed, transcendentals=0
        ),
    )(*args)


def shape(dims, kind=F32):
    return jax.ShapeDtypeStruct(dims, kind)


def counts(code):
    rows = lax.broadcasted_iota(jnp.int32, (T, T), 0)
    cols = lax.broadcasted_iota(jnp.int32, (T, T), 1)
    lower = jnp.where(rows >= cols, 1.0, 0.0).astype(BF16)
    pad = jnp.zeros((126, T), F32)
    high = jnp.concatenate([(code >> 8).astype(F32), pad], axis=0).astype(BF16)
    low = jnp.concatenate([(code & 255).astype(F32), pad], axis=0).astype(BF16)
    return lower, high, low, 256.0 * nt(lower, high) + nt(lower, low)


def both_counts(code):
    rows = lax.broadcasted_iota(jnp.int32, (T, T), 0)
    cols = lax.broadcasted_iota(jnp.int32, (T, T), 1)
    upper = jnp.where(rows <= cols, 1.0, 0.0).astype(BF16)
    _, high, low, count = counts(code)
    return rows, cols, count, 256.0 * nn(high, upper) + nn(low, upper)


def payload_kernel(
    rate_ref, weight_ref, x_ref, inj_ref, code_ref, state_ref, pay_ref, chain_ref, sem,
):
    core = lax.rem(lax.axis_index("dp"), 2)
    half = weight_ref.at[:, pl.ds(pl.multiple_of(core * 512, 512), 512)]
    copy = fetch(half, pay_ref.at[pl.ds(0, HP), :], sem)
    count = counts(code_ref[...])[3]
    inject_f = inj_ref[...].astype(F32)
    for h in range(2):
        rate = rate_ref[h]
        x = x_ref[:, h * 128 : h * 128 + 128]
        end = count[T - 1 :, h : h + 1]
        span = -rate * (end - count[:, h : h + 1])
        b_hi, b_lo = split(span * jnp.exp(span) * inject_f)
        cum_end = -rate * end
        end_w = jnp.exp(cum_end)
        chain = tn(x, b_hi) + tn(x, b_lo) + (cum_end * end_w) * state_ref[h]
        chain_ref[h, :N, :] = chain
        chain_ref[h, N:, :] = jnp.broadcast_to(end_w, (8, 128))
        for k, term in enumerate(split(chain_ref[h])):
            at = (2 * k + h) * 128
            pay_ref[HP : HP + N + 8, at : at + 128] = term
    copy.wait()


def forward_kernel(rate_ref, x_ref, inj_ref, rd_ref, code_ref, state_ref, out_t_ref, mix_ref):
    rows, cols, count, count_t = both_counts(code_ref[...])
    inject = inj_ref[...]
    read = rd_ref[...]
    for h in range(2):
        rate = rate_ref[h]
        hs = slice(h * 128, h * 128 + 128)
        x = x_ref[:, hs]
        s_hi, s_lo = split(state_ref[h])
        start_w = jnp.exp(-rate * count[:, h : h + 1])
        carried = (nt(read, s_hi) + nt(read, s_lo)) * start_w
        for i in range(T // ROWS):
            rs = slice(i * ROWS, i * ROWS + ROWS)
            width = (i + 1) * ROWS
            inter = nt(read[rs], inject[:width])
            spread = -rate * (count[rs, h : h + 1] - count_t[h : h + 1, :width])
            keep = rows[rs, :width] >= cols[rs, :width]
            wts = jnp.where(keep, jnp.exp(jnp.where(keep, spread, 0.0)), 0.0)
            narrow = (inter * wts).astype(BF16)
            mix_ref[h, rs, :width] = narrow
            out_t_ref[hs, rs] = (nn(narrow, x[:width]) + carried[rs]).T.astype(BF16)


def prepare_kernel(
    rate_ref, x_ref, inj_ref, rd_ref, code_ref, state_ref, wts_ref, part_ref, fr_ref, aux_ref,
):
    rows, cols, count, count_t = both_counts(code_ref[...])
    inject = inj_ref[...]
    read = rd_ref[...]
    read_f = read.astype(F32)
    lane = lax.broadcasted_iota(jnp.int32, (T, 128), 1)
    aux = jnp.zeros((T, 128), F32)
    for h in range(2):
        rate = rate_ref[h]
        hs = slice(h * 128, h * 128 + 128)
        x = x_ref[:, hs]
        s_hi, s_lo = split(state_ref[h])
        cum = -rate * count[:, h : h + 1]
        start_w = jnp.exp(cum)
        to_end = jnp.exp(-rate * (count[T - 1 :, h : h + 1] - count[:, h : h + 1]))
        aux = jnp.where(lane == h, to_end, aux)
        aux = jnp.where(lane == 2 + h, start_w, aux)
        fr_ref[h] = (start_w * read_f).astype(BF16)
        weighted = (nt(read, s_hi) + nt(read, s_lo)) * (start_w * cum)
        for i in range(T // ROWS):
            rs = slice(i * ROWS, i * ROWS + ROWS)
            width = (i + 1) * ROWS
            inter = nt(read[rs], inject[:width])
            spread = -rate * (count[rs, h : h + 1] - count_t[h : h + 1, :width])
            keep = rows[rs, :width] >= cols[rs, :width]
            spread = jnp.where(keep, spread, 0.0)
            wts = jnp.where(keep, jnp.exp(spread), 0.0)
            wts_ref[h, rs, :width] = wts.astype(BF16)
            r_hi, r_lo = split(inter * wts * spread)
            part_ref[rs, hs] = weighted[rs] + nn(r_hi, x[:width]) + nn(r_lo, x[:width])
    aux_ref[...] = aux


def fetch(source, target, sem):
    copy = pltpu.make_async_copy(source, target, sem)
    copy.start()
    return copy


def weight_kernel(out_t_ref, cot_ref, send_ref, keep_ref):
    core = lax.rem(lax.axis_index("dp"), 2)
    for k in range(PLANE // WEIGHT_STEPS):
        for ref, side in ((send_ref, 1 - core), (keep_ref, core)):
            block = cot_ref[:, pl.ds(pl.multiple_of((2 * k + side) * 256, 256), 256)]
            ref[k] = nn(out_t_ref[...], block).astype(BF16)


def gridded(kernel, steps, in_specs, out_specs, outs, args, scratch=(), limit=VMEM_LIMIT):
    return pl.pallas_call(
        kernel,
        out_shape=outs,
        grid_spec=pltpu.PrefetchScalarGridSpec(
            num_scalar_prefetch=1,
            grid=(steps,),
            in_specs=in_specs,
            out_specs=out_specs,
            scratch_shapes=scratch,
        ),
        compiler_params=pltpu.CompilerParams(vmem_limit_bytes=limit),
        cost_estimate=pl.CostEstimate(flops=0, bytes_accessed=0, transcendentals=0),
    )(*args)


def fixed(dims):
    return pl.BlockSpec(dims, lambda i, place: (0,) * len(dims))


def core_sum_kernel(place_ref, kept_a, recv_a, kept_b, recv_b, *outs):
    rows = (kept_a[0].astype(F32) + recv_a[0].astype(F32)).astype(BF16)
    cols = (kept_b[:, 0].astype(F32) + recv_b[:, 0].astype(F32)).astype(BF16)
    for d in range(SIDE):

        @pl.when(pl.program_id(0) == d)
        def _(d=d):
            outs[d][...] = rows
            outs[SIDE + d][...] = cols


def line_sum_kernel(place_ref, *refs):
    ins, outs = refs[:8], refs[8:]
    for part in range(2):
        mine = place_ref[3 - part]
        for d in range(SIDE):
            at = lax.rem(mine + d, SIDE)
            total = ins[part * 4][at].astype(F32)
            for j in range(1, SIDE):
                total = total + ins[part * 4 + j][at].astype(F32)
            outs[part * 4 + d][...] = total


def plane_sum_kernel(*refs):
    ins, out_ref = refs[:8], refs[8]
    for part in range(2):
        total = ins[part * 4][...] + ins[part * 4 + 1][...]
        total = total + ins[part * 4 + 2][...] + ins[part * 4 + 3][...]
        for k in range(4):
            out_ref[part * 4 + k] = total[k * 32 : k * 32 + 32, :]


def rate_vector_kernel(
    place_ref, part_ref, rd_ref, aux_ref, gathered_ref, o_ref, later_ref, all_ref, sem,
):
    fetch(gathered_ref.at[:, pl.ds(HP, N + 8), :], all_ref, sem).wait()
    for h in range(2):
        hs = slice(h * 128, h * 128 + 128)
        low = slice(256 + h * 128, 384 + h * 128)
        running = jnp.zeros((N, 128), F32)
        for c in range(DEPTH):
            term = all_ref[c, :, hs].astype(F32) + all_ref[c, :, low].astype(F32)
            decay = term[N : N + 1, :]
            later_ref[c, 8 * h : 8 * h + 8, :] = term[N:, :]
            running = jnp.where(c < place_ref[1], term[:N] + decay * running, running)
        q_hi, q_lo = split(running)
        through = nt(rd_ref[...], q_hi) + nt(rd_ref[...], q_lo)
        o_ref[:, hs] = part_ref[:, hs] + aux_ref[:, 2 + h : 3 + h] * through


def output_grad_kernel(
    place_ref, cot_ref, mine_ref, other_ref, fr_ref, vec_ref, og_ref, pay_ref, acc,
):
    core = place_ref[0]
    step = pl.program_id(0)
    total = None
    for k in range(4):
        first = cot_ref[:, pl.ds(pl.multiple_of((2 * k + core) * 512, 512), 512)]
        second = cot_ref[:, pl.ds(pl.multiple_of((2 * k + 1 - core) * 512, 512), 512)]
        terms = nt(first, mine_ref[k]) + nt(second, other_ref[k])
        total = terms if total is None else total + terms

    @pl.when(step == 0)
    def _():
        acc[...] = total

    @pl.when(step > 0)
    def _():
        acc[...] += total

    @pl.when(step == pl.num_programs(0) - 1)
    def _():
        grad = acc[...].astype(BF16)
        og_ref[...] = grad
        tail = []
        for h in range(2):
            hs = slice(h * 128, h * 128 + 128)
            narrow = tn(grad[:, hs], fr_ref[h]).astype(BF16)
            for z in range(DEPTH):
                pay_ref[z, hs, :] = narrow
            rate = jnp.sum(grad[:, hs].astype(F32) * vec_ref[:, hs], axis=0, keepdims=True)
            rest = jnp.broadcast_to(jnp.sum(rate, axis=1, keepdims=True), (8, 128))
            rest_row = lax.broadcasted_iota(jnp.int32, (8, 128), 0)
            terms = jnp.zeros((8, 128), F32)
            for k in range(3):
                term = rest.astype(BF16).astype(F32)
                terms = jnp.where(rest_row == k, term, terms)
                rest = rest - term
            tail.append(terms)
        tail = jnp.concatenate(tail, axis=0).astype(BF16)
        for z in range(DEPTH):
            pay_ref[z, HP:, :] = tail


def backward_kernel(
    g_ref, x_ref, inj_ref, rd_ref, state_ref, mix_ref, wts_ref, aux_ref, gi_ref, ginj_ref,
    gread_ref,
):
    inject = inj_ref[...]
    read = rd_ref[...]
    gi_ref[...] = jnp.zeros((T, HP), F32)
    ginj_ref[...] = jnp.zeros((T, N), F32)
    for h in range(2):
        hs = slice(h * 128, h * 128 + 128)
        x = x_ref[:, hs]
        g = g_ref[:, hs]
        state = state_ref[h].astype(BF16)
        for i in range(T // ROWS):
            rs = slice(i * ROWS, i * ROWS + ROWS)
            width = (i + 1) * ROWS
            pairing = (nt(g[rs], x[:width]) * wts_ref[h, rs, :width].astype(F32)).astype(BF16)
            through = nn(g[rs], state) * aux_ref[rs, 2 + h : 3 + h]
            read_part = nn(pairing, inject[:width]) + through
            if h == 0:
                gread_ref[rs, :] = read_part
            else:
                gread_ref[rs, :] += read_part
            ginj_ref[:width, :] += tn(pairing, read[rs])
            gi_ref[:width, hs] += tn(mix_ref[h, rs, :width], g[rs])


def finish_kernel(
    place_ref, gi_ref, ginj_ref, x_ref, inj_ref, aux_ref, adj_ref, decay_ref, o_gi_ref, o_ginj_ref,
):
    total = ginj_ref[...]
    inject = inj_ref[...]
    for h in range(2):
        hs = slice(h * 128, h * 128 + 128)
        running = jnp.zeros((128, N), F32)
        for c in range(DEPTH - 1, 0, -1):
            decay = decay_ref[c, 8 * h : 8 * h + 1, :]
            later = adj_ref[c, hs, :].astype(F32) + decay * running
            running = jnp.where(c > place_ref[1], later, running)
        incoming = running.astype(BF16)
        to_end = aux_ref[:, h : h + 1]
        o_gi_ref[:, hs] = (gi_ref[:, hs] + to_end * nt(inject, incoming)).astype(BF16)
        total = total + to_end * nn(x_ref[:, hs], incoming)
    o_ginj_ref[...] = total


def swap_cores(value):
    return lax.ppermute(value, "dp", [(i, i ^ 1) for i in range(2 * PLANE)])


def local(
    cotangent, out_weight, head_input, injector, readout, decay_code, decay_rate, start_state
):
    cot = cotangent[0]
    x = head_input[0]
    inject = injector[0]
    read = readout[0]
    state = start_state[0, 0]
    code = decay_code[0]
    core = lax.axis_index("dp") % 2
    me = lax.axis_index("dp")
    place = jnp.stack([core, lax.axis_index("ctx"), me // 8, me // 2 % SIDE]).astype(jnp.int32)

    pay, chain = call(
        payload_kernel, [shape((HP + N + 8, 512), BF16), shape((2, N + 8, 128))],
        (decay_rate, out_weight, x, inject, code.T, state), smem=(0,), hbm=(1,),
        scratch=[pltpu.SemaphoreType.DMA],
    )
    gathered = lax.all_gather(pay, "ctx", axis=0)
    x, _ = lax.optimization_barrier((x, chain))
    out_t, mix = call(
        forward_kernel, [shape((HP, T), BF16), shape((2, T, T), BF16)],
        (decay_rate, x, inject, read, code.T, state), smem=(0,),
    )
    half_terms = shape((PLANE, 256, 256), BF16)
    width = D // WEIGHT_STEPS
    part_spec = pl.BlockSpec((PLANE // WEIGHT_STEPS, 256, 256), lambda i: (i, 0, 0))
    sent, kept = pl.pallas_call(
        weight_kernel,
        grid=(WEIGHT_STEPS,),
        out_shape=[half_terms, half_terms],
        in_specs=[
            pl.BlockSpec((HP, T), lambda i: (0, 0)),
            pl.BlockSpec((T, width), lambda i: (0, i)),
        ],
        out_specs=[part_spec, part_spec],
        compiler_params=pltpu.CompilerParams(vmem_limit_bytes=VMEM_LIMIT),
        cost_estimate=pl.CostEstimate(flops=0, bytes_accessed=0, transcendentals=0),
    )(out_t, cot)
    parts = core_sum(place, kept, swap_cores(sent))
    first = exchanged(parts[:SIDE], 8)
    second = exchanged(parts[SIDE:], 2)
    parts = call(line_sum_kernel, [shape((128, 256))] * 8, (place, *first, *second), smem=(0,), limit=16 << 20)

    read_later, _ = lax.optimization_barrier((read, kept))
    wts, part, from_start, aux = call(
        prepare_kernel,
        [shape((2, T, T), BF16), shape((T, HP)), shape((2, T, N), BF16), shape((T, 128))],
        (decay_rate, x, inject, read_later, code.T, state), smem=(0,),
    )

    gathered, _ = lax.optimization_barrier((gathered, (parts, aux)))
    mine = gathered[:, :HP, :]
    other = swap_cores(mine)
    vector, decay = call(
        rate_vector_kernel, [shape((T, HP)), shape((DEPTH, 16, 128))],
        (place, part, read, aux, gathered), smem=(0,), hbm=(4,),
        scratch=[pltpu.VMEM((DEPTH, N + 8, 512), BF16), pltpu.SemaphoreType.DMA],
    )
    one = pl.BlockSpec((4, HP, 512), lambda i, place: (i, 0, 0))
    grad, pay = gridded(
        output_grad_kernel, 2,
        [
            pl.BlockSpec((T, 4096), lambda i, place: (0, i)), one, one, fixed((2, T, N)),
            fixed((T, HP)),
        ],
        [fixed((T, HP)), fixed((DEPTH, HP + 16, 128))],
        [shape((T, HP), BF16), shape((DEPTH, HP + 16, 128), BF16)],
        (place, cot, mine, other, from_start, vector), [pltpu.VMEM((T, HP), F32)],
    )
    parts, _ = lax.optimization_barrier((parts, pay))
    first = exchanged(parts[:SIDE], 2)
    second = exchanged(parts[SIDE:], 8)
    pay = lax.all_to_all(pay, "ctx", 0, 0, tiled=True)
    gi, ginj, grad_read = call(
        backward_kernel, [shape((T, HP)), shape((T, N)), shape((T, N))],
        (grad, x, inject, read, state, mix, wts, aux),
    )
    first[1:], _ = lax.optimization_barrier((first[1:], gi))
    blocks = call(plane_sum_kernel, shape((DEPTH, 32, 256)), (*first, *second), limit=16 << 20)
    blocks, pay = lax.optimization_barrier((blocks, pay))
    blocks = lax.all_to_all(blocks, "ctx", 0, 0, tiled=True)
    rate = jnp.sum(pay[:, HP:, :].astype(F32).reshape(DEPTH, 2, 8, 128), axis=(0, 2))
    rate = plane_total(rate)
    grad_input, grad_inject = call(
        finish_kernel, [shape((T, HP), BF16), shape((T, N))],
        (place, gi, ginj, x, inject, aux, pay, decay), smem=(0,), limit=16 << 20,
    )
    grad_weight = jnp.sum(blocks, axis=0)
    tokens = T * lax.axis_size("dp") * lax.axis_size("ctx")
    return grad_input[None], grad_inject[None], grad_read[None], grad_weight, rate[:, 0] / tokens


def core_sum(place, kept, recv):
    kept, recv = (a.reshape(SIDE, SIDE, 256, 256) for a in (kept, recv))
    by_x = pl.BlockSpec(
        (1, SIDE, 128, 256), lambda d, place: (lax.rem(place[2] + d, SIDE), 0, 0, 0)
    )
    by_y = pl.BlockSpec(
        (SIDE, 1, 128, 256), lambda d, place: (0, lax.rem(place[3] + d, SIDE), 1, 0)
    )
    part = (SIDE, 128, 256)
    return gridded(
        core_sum_kernel, SIDE, [by_x, by_x, by_y, by_y], [fixed(part)] * 8,
        [shape(part, BF16)] * 8, (place, kept, recv, kept, recv), limit=16 << 20,
    )


def exchanged(parts, unit):
    def pairs(d):
        def target(i):
            at = i // unit % SIDE
            return i + ((at + d) % SIDE - at) * unit

        return [(i, target(i)) for i in range(2 * PLANE)]

    return [parts[0]] + [lax.ppermute(parts[d], "dp", pairs(d)) for d in range(1, SIDE)]


def flipped(value, bits):
    return lax.ppermute(value, "dp", [(i, i ^ bits) for i in range(2 * PLANE)])


def plane_total(value):
    value = value + flipped(value, 1)
    for unit in (2, 8):
        one, two, three = (flipped(value, unit * k) for k in (1, 2, 3))
        value = (value + two) + (one + three)
    return value


def solution(mesh):
    in_specs = (
        P("dp", "ctx", None),
        P(None, "ctx"),
        P("dp", "ctx", None),
        P("dp", "ctx", None),
        P("dp", "ctx", None),
        P("dp", "ctx", None),
        P(),
        P("dp", "ctx", None, None, None),
    )
    out_specs = (
        P("dp", "ctx", None),
        P("dp", "ctx", None),
        P("dp", "ctx", None),
        P("ctx", "dp"),
        P(),
    )
    return jax.shard_map(local, mesh=mesh, in_specs=in_specs, out_specs=out_specs, check_vma=False)
```
